256 devices in a mesh: lon: 16 (over x, y_lo, core), dates: 16 (over z, y_hi).
Axes of the slice: x: 4, y: 4 (y_hi: 2, y_lo: 2; y = y_hi * 2 + y_lo), z: 8, core: 2. Of those that a mesh axis runs over, the one named last changes fastest.
Arguments:
- features: bfloat16 [16, 4096, 1024], P('dates', 'lon'), may hold values from -24 to 24
- w_qkv: bfloat16 [1024, 3072], replicated, may hold values from -2 to 2
- grad_out: bfloat16 [16, 4096, 1024], P('dates', 'lon'), may hold values from -6 to 6
- positions: int32 [16, 4096], P('dates', 'lon'), may hold values from 0 to 4095, as said below
- block_list: int32 [16, 5], P('dates'), may hold values from -2 to 2, as said below
Outputs:
- attn_out: bfloat16 [16, 4096, 1024], P('dates', 'lon')
- grad_x: bfloat16 [16, 4096, 1024], P('dates', 'lon')
- grad_w: float32 [1024, 3072], P('dates', 'lon')
The draws below stay inside these ranges and needn't reach their ends.
Inputs may be any that keep to these rules, and one draw needn't show every extreme that they name: `positions`: positions never fall along a sample's row. `block_list`: each sample's list holds 0 and every offset from -r to r for its reach r of 0 to 2; other entries are 0; some sample has reach 2.
All inputs are finite; a program needn't handle non-finite values.
Results may differ from the reference program's by a relative error of at most 0.034.
Values may be sent and summed in bfloat16 or wider, within the bound.
A program may use at most 128 MiB of HBM per device.

```python
import jax
import jax.numpy as jnp
from jax import lax

D = 1024
HEADS = 16
LON_DEV = 256
W_MAX = 2
LAT_ROWS = 64
B = 16
LON = 4096
N_LON = 16


def row_layout(key):
    latitude = jax.random.randint(jax.random.fold_in(key, 11), (B,), 0, LAT_ROWS)
    latitude = latitude.at[0].set(0).at[1].set(LAT_ROWS - 1)
    reach_blocks = W_MAX - latitude * (W_MAX + 1) // LAT_ROWS
    stride = 1 + latitude * 4 // LAT_ROWS
    return (reach_blocks, stride)


def draw_block_list(key, part):
    reach_blocks, stride = row_layout(key)
    offsets = jnp.arange(2 * W_MAX + 1, dtype=jnp.int32) - W_MAX
    chosen = jnp.abs(offsets)[None, :] <= reach_blocks[:, None]
    return jnp.where(chosen, offsets[None, :], 0).astype(jnp.int32)


def draw_positions(key, part):
    reach_blocks, stride = row_layout(key)
    longitude = jnp.arange(LON, dtype=jnp.int32)
    return (longitude[None, :] * stride[:, None] // 4).astype(jnp.int32)


def draw_w_qkv(key, part):
    shape_pair = (D, D)
    query_part = jax.random.truncated_normal(jax.random.fold_in(key, 21), -4.0, 4.0, shape_pair, jnp.float32) * D ** (-0.5)
    key_part = jax.random.truncated_normal(jax.random.fold_in(key, 22), -4.0, 4.0, shape_pair, jnp.float32) * D ** (-0.5)
    value_part = jax.random.truncated_normal(jax.random.fold_in(key, 23), -4.0, 4.0, shape_pair, jnp.float32) * D ** (-0.5)
    key_cols = key_part
    return jnp.concatenate([query_part, key_cols, value_part], axis=1).astype(jnp.bfloat16)


def draw_features(key, part):
    normal_part = jax.random.truncated_normal(jax.random.fold_in(key, 31), -4.0, 4.0, (B, LON, D), jnp.float32)
    result = normal_part
    return result.astype(jnp.bfloat16)


def shard_levels(stream_key, shape, split, least, largest):
    gain = 1.0
    for position, shards_of in split:
        steps = jax.random.uniform(jax.random.fold_in(jax.random.fold_in(stream_key, 6), position), (shards_of,), jnp.float32, least / len(split), largest / len(split))
        gain = gain * jnp.repeat(jnp.exp(steps), shape[position] // shards_of).reshape((-1,) + (1,) * (len(shape) - 1 - position))
    return gain


def bell_draw(rng, extent, deviation, bound, pieces=(), kind=jnp.bfloat16):
    loudness = shard_levels(rng, extent, pieces, -0.22, 0.18) if pieces else 1.0
    array = jax.random.normal(rng, extent, jnp.float32) * deviation * loudness
    return jnp.minimum(jnp.maximum(array, -bound), bound).astype(kind)


def setup_inputs(seed: int = 0) -> dict:
    streams_of = jax.random.split(jax.random.key(seed), 6)
    return {
        "features": draw_features(jax.random.fold_in(streams_of[5], 71), 0),
        "w_qkv": draw_w_qkv(jax.random.fold_in(streams_of[5], 71), 0),
        "grad_out": bell_draw(streams_of[2], (B, LON, D), 1.0, 6.0, ((0, 16), (1, 16))),
        "positions": draw_positions(jax.random.fold_in(streams_of[5], 71), 0),
        "block_list": draw_block_list(jax.random.fold_in(streams_of[5], 71), 0),
    }


INTERP = 0.25
BASE = 10000.0
NEG_FILL = -1e30


def rope_tables(row_positions, head_dim):
    pair_index = jnp.arange(head_dim // 2, dtype=jnp.float32)
    frequency = INTERP * BASE ** (-2.0 * pair_index / head_dim)
    angles = row_positions.astype(jnp.float32)[..., None] * frequency
    return jnp.cos(angles)[..., None, :], jnp.sin(angles)[..., None, :]


def rotate(values, cosine, sine_table):
    half_dim = values.shape[-1] // 2
    first_half = values[..., :half_dim]
    second_half = values[..., half_dim:]
    return jnp.concatenate([first_half * cosine - second_half * sine_table, first_half * sine_table + second_half * cosine], axis=-1)


def unrotate(values, cosine, sine_table):
    half_dim = values.shape[-1] // 2
    first_half = values[..., :half_dim]
    second_half = values[..., half_dim:]
    return jnp.concatenate([first_half * cosine + second_half * sine_table, second_half * cosine - first_half * sine_table], axis=-1)


def low_round(values):
    return lax.optimization_barrier(values.astype(jnp.bfloat16)).astype(jnp.float32)


def reference(features, w_qkv, grad_out, positions, block_list):
    head_dim = D // HEADS
    score_scale = head_dim ** -0.5
    offsets = jnp.arange(-W_MAX, W_MAX + 1, dtype=jnp.int32)
    factor = (B * LON) ** -0.5
    block_dimensions = (N_LON, LON_DEV, HEADS, head_dim)
    head_shape = (LON, HEADS, head_dim)

    def one_sample(weight_sum, sample):
        tokens, upstream, row_positions, listing = sample
        projected = jnp.dot(tokens, w_qkv, preferred_element_type=jnp.float32)
        cosine, sine_table = rope_tables(row_positions, head_dim)
        query = rotate(projected[:, :D].reshape(head_shape), cosine, sine_table).astype(jnp.bfloat16)
        key_row_stack = rotate(projected[:, D:2 * D].reshape(head_shape), cosine, sine_table).astype(jnp.bfloat16)
        values = projected[:, 2 * D:].astype(jnp.bfloat16).reshape(head_shape)
        used_slots = jnp.any(listing[None, :] == offsets[:, None], axis=1)
        query_blocks = query.reshape(block_dimensions)
        key_blocks = key_row_stack.reshape(block_dimensions)
        value_blocks = values.reshape(block_dimensions)
        upstream_blocks = upstream.reshape(block_dimensions)
        mask = used_slots[None, None, :, None]

        def one_block(carry_sums, block_index):
            grad_keys, grad_values = carry_sums
            near_blocks = ((block_index + offsets) % N_LON).astype(jnp.int32)
            query_block = query_blocks[block_index].astype(jnp.float32)
            key_near = key_blocks[near_blocks].astype(jnp.float32)
            value_near = value_blocks[near_blocks].astype(jnp.float32)
            grad_block = upstream_blocks[block_index].astype(jnp.float32)
            scores = jnp.einsum('qhd,skhd->hqsk', query_block, key_near) * score_scale
            scores = jnp.where(mask, scores, NEG_FILL)
            row_max = jnp.max(scores, axis=(2, 3), keepdims=True)
            exp_scores = jnp.where(mask, jnp.exp(scores - row_max), 0.0)
            totals = jnp.sum(exp_scores, axis=(2, 3), keepdims=True)
            attn_probs = exp_scores / totals
            reduced_probabilities = low_round(attn_probs)
            out_block = jnp.einsum('hqsk,skhd->qhd', reduced_probabilities, value_near).astype(jnp.bfloat16)
            row_delta = jnp.sum(grad_block * lax.optimization_barrier(out_block).astype(jnp.float32), axis=-1)
            dprobs = jnp.einsum('qhd,skhd->hqsk', grad_block, value_near)
            score_gradient = low_round(attn_probs * (dprobs - row_delta.T[:, :, None, None]))
            dquery = score_scale * jnp.einsum('hqsk,skhd->qhd', score_gradient, key_near)
            key_grads = score_scale * jnp.einsum('hqsk,qhd->skhd', score_gradient, query_block)
            value_grads = jnp.einsum('hqsk,qhd->skhd', reduced_probabilities, grad_block)
            new_sums = (grad_keys.at[near_blocks].add(key_grads), grad_values.at[near_blocks].add(value_grads))
            return new_sums, (out_block, dquery)

        zero_grads = jnp.zeros(block_dimensions, jnp.float32)
        (grad_keys, grad_values), (out_blocks, dquery_all) = lax.scan(one_block, (zero_grads, zero_grads), jnp.arange(N_LON, dtype=jnp.int32))
        attn_rows = out_blocks.reshape(LON, D)
        dquery_full = unrotate(dquery_all.reshape(head_shape), cosine, sine_table)
        dkey_full = unrotate(grad_keys.reshape(head_shape), cosine, sine_table)
        dqkv = jnp.concatenate([dquery_full.reshape(LON, D), dkey_full.reshape(LON, D), grad_values.reshape(LON, D)], axis=1).astype(jnp.bfloat16)
        grad_rows = jnp.dot(dqkv, w_qkv.T, preferred_element_type=jnp.float32).astype(jnp.bfloat16)
        weight_term = jnp.dot(tokens.T, dqkv, preferred_element_type=jnp.float32)
        return weight_sum + weight_term, (attn_rows, grad_rows)

    zero_weight = jnp.zeros((D, 3 * D), jnp.float32)
    weight_sum, (attn_out, grad_x) = lax.scan(one_sample, zero_weight, (features, grad_out, positions, block_list))
    return attn_out, grad_x, weight_sum * factor
```

```python
import functools

import jax
import jax.numpy as jnp
from jax import lax
from jax.experimental import pallas as pl
from jax.experimental.pallas import tpu as pltpu
from jax.sharding import PartitionSpec as P

HEADS = 16
W_MAX = 2
INTERP = 0.25
BASE = 10000.0
FAR = 1e30
LOG2E = 1.4426950408889634
BF = jnp.bfloat16
F32 = jnp.float32
MESH = pl.DeviceIdType.MESH
N_LON = 16
ROWS = 256
GROUPS = 4
SLOTS = 5


def dot(a, b):
    return lax.dot_general(a, b, (((1,), (0,)), ((), ())), preferred_element_type=F32)


def dot_t(a, b):
    return lax.dot_general(a, b, (((1,), (1,)), ((), ())), preferred_element_type=F32)


def lanes(shape):
    return lax.broadcasted_iota(jnp.int32, shape, len(shape) - 1)


def perm_matrix():
    source = lax.broadcasted_iota(jnp.int32, (256, 256), 0)
    column = lax.broadcasted_iota(jnp.int32, (256, 256), 1)
    wanted = (column // 32 % 4) * 64 + (column // 128) * 32 + column % 32
    return jnp.where(source == wanted, 1.0, 0.0).astype(BF)


def turn(value, cosine, sine):
    a, c = value[:, :128], value[:, 128:]
    return jnp.concatenate([a * cosine - c * sine, a * sine + c * cosine], axis=1)


def turn_back(value, cosine, sine):
    a, c = value[:, :128], value[:, 128:]
    return jnp.concatenate([a * cosine + c * sine, c * cosine - a * sine], axis=1)


def query_kernel(bias_ref, x_ref, wq_ref, wk_ref, wv_ref, cos_ref, sin_ref, up_ref,
                 out_ref, dq_ref, q_ref, k_ref, v_ref, stats_ref, kbuf, vbuf, stats):
    group = pl.program_id(0)
    perm = perm_matrix()
    wq = dot(wq_ref[...], perm).astype(BF)
    wk = dot(wk_ref[...], perm).astype(BF)
    wv = wv_ref[...]
    for slot in range(SLOTS):
        x = x_ref[slot]
        cosine, sine = cos_ref[slot], sin_ref[slot]
        rows = slice(slot * ROWS, (slot + 1) * ROWS)
        q_ref[rows] = (turn(dot(x, wq), cosine, sine).astype(BF).astype(F32) * 0.125).astype(BF)
        kbuf[rows] = turn(dot(x, wk), cosine, sine).astype(BF)
        vbuf[rows] = dot(x, wv).astype(BF)
    k_ref[...] = kbuf[:ROWS]
    v_ref[...] = vbuf[:ROWS]
    lane = lanes((ROWS, 256))
    lane_pair = lane // 32 % 4
    lane_flat = lane // 64
    stat_lane = lanes((ROWS, 128))
    query = q_ref[:ROWS]
    up = up_ref[...]
    zero = jnp.zeros((), BF)
    out = jnp.zeros((ROWS, 256), F32)
    dquery = jnp.zeros((ROWS, 256), F32)

    @pl.when(group == 0)
    def _():
        stats[...] = jnp.zeros_like(stats)

    for head in range(4):
        own_pair = lane_pair == head
        own_flat = lane_flat == head
        scores = dot_t(jnp.where(own_pair, query, zero), kbuf[...]) * LOG2E
        row_max = None
        for slot in range(SLOTS):
            one = jnp.max(scores[:, slot * ROWS:(slot + 1) * ROWS], axis=1, keepdims=True) - bias_ref[0, slot]
            row_max = one if row_max is None else jnp.maximum(row_max, one)
        parts = []
        total = None
        for slot in range(SLOTS):
            one = jnp.exp2(scores[:, slot * ROWS:(slot + 1) * ROWS] - (row_max + bias_ref[0, slot]))
            part_sum = jnp.sum(one, axis=1, keepdims=True)
            total = part_sum if total is None else total + part_sum
            parts.append(one)
        weights = jnp.concatenate(parts, axis=1)
        inverse = 1.0 / total
        attended = dot(weights.astype(BF), vbuf[...]) * inverse
        attended = attended.astype(BF).astype(F32)
        out = jnp.where(own_flat, attended, out)
        up_own = jnp.where(own_flat, up, zero)
        delta = jnp.sum(up_own.astype(F32) * attended, axis=1, keepdims=True)
        dprobs = dot_t(up_own, vbuf[...])
        dscores = (weights * (dprobs - delta)).astype(BF)
        dquery = jnp.where(own_pair, dot(dscores, kbuf[...]) * (inverse * 0.125), dquery)
        index = group * 4 + head
        now = stats[...]
        now = jnp.where(stat_lane == index, row_max + jnp.log2(total), now)
        stats[...] = jnp.where(stat_lane == index + HEADS, delta, now)
    out_ref[...] = out.astype(BF)
    dquery = turn_back(dquery, cos_ref[0], sin_ref[0]).astype(BF)
    dq_ref[...] = dot_t(dquery, perm).astype(BF)

    @pl.when(group == GROUPS - 1)
    def _():
        stats_ref[...] = stats[...].T[:2 * HEADS]


def key_kernel(lse_ref, delta_ref, q_ref, up_ref, k_ref, v_ref, cos_ref, sin_ref, dk_ref, dv_ref):
    group = pl.program_id(0)
    perm = perm_matrix()
    lane = lanes((ROWS, 256))
    lane_pair = lane // 32 % 4
    lane_flat = lane // 64
    zero = jnp.zeros((), BF)
    key, value = k_ref[...], v_ref[...]
    dkey = jnp.zeros((ROWS, 256), F32)
    dvalue = jnp.zeros((ROWS, 256), F32)
    for head in range(4):
        own_pair = lane_pair == head
        own_flat = lane_flat == head
        lse = lse_ref[pl.ds(group * 4 + head, 1), :]
        delta = delta_ref[pl.ds(group * 4 + head, 1), :]
        scores = dot_t(jnp.where(own_pair, key, zero), q_ref[...]) * LOG2E
        probs = jnp.exp2(scores - lse)
        dprobs = dot_t(jnp.where(own_flat, value, zero), up_ref[...])
        dscores = (probs * (dprobs - delta)).astype(BF)
        dvalue = jnp.where(own_flat, dot(probs.astype(BF), up_ref[...]), dvalue)
        dkey = jnp.where(own_pair, dot(dscores, q_ref[...]), dkey)
    dkey = turn_back(dkey, cos_ref[...], sin_ref[...]).astype(BF)
    dk_ref[...] = dot_t(dkey, perm).astype(BF)
    dv_ref[...] = dvalue.astype(BF)


def run_query(bias, x5, w, cos5, sin5, up):
    full = lambda *shape: pl.BlockSpec(shape, lambda g: (0,) * len(shape))
    col = lambda rows: pl.BlockSpec((rows, 256), lambda g: (0, g))
    bf = lambda rows: jax.ShapeDtypeStruct((rows, 1024), BF)
    return pl.pallas_call(
        query_kernel,
        grid=(GROUPS,),
        in_specs=[
            pl.BlockSpec(memory_space=pltpu.SMEM),
            full(SLOTS, ROWS, 1024),
            pl.BlockSpec((1024, 256), lambda g: (0, g)),
            pl.BlockSpec((1024, 256), lambda g: (0, g + 4)),
            pl.BlockSpec((1024, 256), lambda g: (0, g + 8)),
            full(SLOTS, ROWS, 128),
            full(SLOTS, ROWS, 128),
            col(ROWS),
        ],
        out_specs=[col(ROWS), col(ROWS), col(SLOTS * ROWS), col(ROWS), col(ROWS), full(2 * HEADS, ROWS)],
        out_shape=[bf(ROWS), bf(ROWS), bf(SLOTS * ROWS), bf(ROWS), bf(ROWS),
                   jax.ShapeDtypeStruct((2 * HEADS, ROWS), F32)],
        scratch_shapes=[pltpu.VMEM((SLOTS * ROWS, 256), BF), pltpu.VMEM((SLOTS * ROWS, 256), BF),
                        pltpu.VMEM((ROWS, 128), F32)],
        compiler_params=pltpu.CompilerParams(vmem_limit_bytes=60 * 2**20),
        cost_estimate=pl.CostEstimate(flops=30 * 10**9, bytes_accessed=12 * 2**20, transcendentals=5 * 2**20),
        name="query_side",
    )(bias, x5, w, w, w, cos5, sin5, up)


def run_key(lse, delta, q5, up5, k, v, cosine, sine):
    full = lambda *shape: pl.BlockSpec(shape, lambda g: (0,) * len(shape))
    col = lambda rows: pl.BlockSpec((rows, 256), lambda g: (0, g))
    bf = lambda rows: jax.ShapeDtypeStruct((rows, 1024), BF)
    return pl.pallas_call(
        key_kernel,
        grid=(GROUPS,),
        in_specs=[full(HEADS, SLOTS * ROWS), full(HEADS, SLOTS * ROWS), col(SLOTS * ROWS), col(SLOTS * ROWS),
                  col(ROWS), col(ROWS), full(ROWS, 128), full(ROWS, 128)],
        out_specs=[col(ROWS), col(ROWS)],
        out_shape=[bf(ROWS), bf(ROWS)],
        compiler_params=pltpu.CompilerParams(vmem_limit_bytes=60 * 2**20),
        cost_estimate=pl.CostEstimate(flops=12 * 10**9, bytes_accessed=8 * 2**20, transcendentals=5 * 2**20),
        name="key_side",
    )(lse, delta, q5, up5, k, v, cosine, sine)


def weight_kernel(x_ref, d_ref, g_ref):
    g_ref[0] = dot(x_ref[...], d_ref[...]).astype(BF)


def run_weight(x_rows, d_both):
    return pl.pallas_call(
        weight_kernel,
        grid=(8,),
        in_specs=[pl.BlockSpec((512, 512), lambda c: (0, 0)), pl.BlockSpec((512, 384), lambda c: (0, c))],
        out_specs=pl.BlockSpec((1, 512, 384), lambda c: (c, 0, 0)),
        out_shape=jax.ShapeDtypeStruct((8, 512, 384), BF),
        name="weight_partial",
    )(x_rows, d_both)


def reduce_kernel(g_ref, o_ref, in_x, in_y, sum_a, sum_b, in_a, in_b, sum_p, in_z, mine, theirs,
                  send_x, recv_x, send_y, recv_y, send_a, recv_a, send_b, recv_b, send_z, recv_z, send_c, recv_c):
    lon, dates = lax.axis_index("lon"), lax.axis_index("dates")
    x, y_lo, core = lon // 4, lon // 2 % 2, lon % 2
    z, y_hi = dates // 2, dates % 2
    y = y_hi * 2 + y_lo

    def at(px, py, pz, pc):
        return {"lon": px * 4 + py % 2 * 2 + pc, "dates": pz * 2 + py // 2}

    x_peers = [lax.rem(x + step, 4) for step in (1, 2, 3)]
    y_peers = [lax.rem(y + step, 4) for step in (1, 2, 3)]
    z_peers = [lax.rem(z + step, 8) for step in range(1, 8)]
    barrier = pltpu.get_barrier_semaphore()
    peers = [at(p, y, z, core) for p in x_peers] + [at(x, p, z, core) for p in y_peers]
    peers += [at(x, y, p, core) for p in z_peers] + [at(x, y, z, 1 - core)]
    for peer in peers:
        pl.semaphore_signal(barrier, inc=1, device_id=peer, device_id_type=MESH)
    pl.semaphore_wait(barrier, len(peers))

    def send(source, target, send_sem, recv_sem, peer):
        copy = pltpu.make_async_remote_copy(src_ref=source, dst_ref=target, send_sem=send_sem, recv_sem=recv_sem,
                                            device_id=peer, device_id_type=MESH)
        copy.start()
        return copy

    first_a = [send(g_ref.at[p, :, pl.ds(0, 4)], in_x.at[i], send_x.at[i], recv_x.at[i], at(p, y, z, core))
               for i, p in enumerate(x_peers)]
    first_b = [send(g_ref.at[:, p % 2, pl.ds(4, 4), p // 2], in_y.at[i], send_y.at[i], recv_y.at[i], at(x, p, z, core))
               for i, p in enumerate(y_peers)]
    for copy in first_a:
        copy.wait()
    for lo in range(2):
        for hi in range(2):
            total = g_ref[x, lo, 0:4, hi].astype(F32)
            for i in range(3):
                total += in_x[i, lo, :, hi].astype(F32)
            sum_a[hi, lo] = total.astype(BF)
    second_a = [send(sum_a.at[p // 2, p % 2], in_a.at[i], send_a.at[i], recv_a.at[i], at(x, p, z, core))
                for i, p in enumerate(y_peers)]
    for copy in first_b:
        copy.wait()
    for px in range(4):
        total = g_ref[px, y_lo, 4:8, y_hi].astype(F32)
        for i in range(3):
            total += in_y[i, px].astype(F32)
        sum_b[px] = total.astype(BF)
    second_b = [send(sum_b.at[p], in_b.at[i], send_b.at[i], recv_b.at[i], at(p, y, z, core))
                for i, p in enumerate(x_peers)]
    for copy in second_a:
        copy.wait()
    total = sum_a[y_hi, y_lo].astype(F32)
    for i in range(3):
        total += in_a[i].astype(F32)
    sum_p[0:4] = total.astype(BF)
    for copy in second_b:
        copy.wait()
    total = sum_b[x].astype(F32)
    for i in range(3):
        total += in_b[i].astype(F32)
    sum_p[4:8] = total.astype(BF)
    third = [send(sum_p.at[p], in_z.at[i], send_z.at[i], recv_z.at[i], at(x, y, p, core))
             for i, p in enumerate(z_peers)]
    for copy in third:
        copy.wait()
    total = sum_p[z].astype(F32)
    for i in range(7):
        total += in_z[i].astype(F32)
    total = total * (65536.0 ** -0.5)
    mine[0] = total[:, :192]
    mine[1] = total[:, 192:]
    last = send(mine.at[1 - core], theirs, send_c, recv_c, at(x, y, z, 1 - core))
    last.wait()
    own = mine[core]
    other = theirs[...]
    o_ref[pl.ds(pl.multiple_of(core * 32, 32), 32), :] = own
    o_ref[pl.ds(pl.multiple_of(32 - core * 32, 32), 32), :] = other


def run_reduce(partial):
    dma = pltpu.SemaphoreType.DMA
    return pl.pallas_call(
        reduce_kernel,
        in_specs=[pl.BlockSpec(memory_space=pltpu.VMEM)],
        out_specs=pl.BlockSpec(memory_space=pltpu.VMEM),
        out_shape=jax.ShapeDtypeStruct((64, 192), F32),
        scratch_shapes=[
            pltpu.VMEM((3, 2, 4, 2, 32, 384), BF),
            pltpu.VMEM((3, 4, 4, 32, 384), BF),
            pltpu.VMEM((2, 2, 4, 32, 384), BF),
            pltpu.VMEM((4, 4, 32, 384), BF),
            pltpu.VMEM((3, 4, 32, 384), BF),
            pltpu.VMEM((3, 4, 32, 384), BF),
            pltpu.VMEM((8, 32, 384), BF),
            pltpu.VMEM((7, 32, 384), BF),
            pltpu.VMEM((2, 32, 192), F32),
            pltpu.VMEM((32, 192), F32),
            dma((3,)), dma((3,)), dma((3,)), dma((3,)), dma((3,)), dma((3,)), dma((3,)), dma((3,)),
            dma((7,)), dma((7,)), dma, dma,
        ],
        compiler_params=pltpu.CompilerParams(collective_id=0, has_side_effects=True, vmem_limit_bytes=40 * 2**20),
        name="weight_reduce",
    )(partial.reshape(4, 2, 8, 2, 32, 384))


SWAP = [(i, i ^ 1) for i in range(N_LON)]
NEAR = [(i, (i + (1 if i % 2 else -1)) % N_LON) for i in range(N_LON)]
WIDE = [(i, (i + (-2 if i % 2 else 2)) % N_LON) for i in range(N_LON)]


def gather_halo(value):
    partner = lax.ppermute(value, "lon", SWAP)
    near = lax.ppermute(value, "lon", NEAR)
    wide = lax.ppermute(value, "lon", WIDE)
    passed = lax.ppermute(near, "lon", SWAP)
    return [value, partner, near, wide, passed]


def per_device(features, w_qkv, grad_out, positions, block_list):
    x, up = features[0], grad_out[0]
    core = lax.axis_index("lon") % 2
    toward = 1 - 2 * core
    offsets = jnp.stack([jnp.int32(0), toward, -toward, -2 * toward, 2 * toward])
    listed = block_list[0]
    used = jnp.any(listed[None, :] == offsets[:, None], axis=1)
    used_by = jnp.any(listed[None, :] == -offsets[:, None], axis=1)
    bias = jnp.where(used, 0.0, FAR).astype(F32).reshape(1, SLOTS)

    pair_index = jnp.arange(32, dtype=F32)
    frequency = INTERP * BASE ** (-2.0 * pair_index / 64)
    spots = jnp.concatenate(gather_halo(positions), axis=0)
    angles = spots.astype(F32)[..., None] * frequency
    cos5 = jnp.tile(jnp.cos(angles), (1, 1, 4))
    sin5 = jnp.tile(jnp.sin(angles), (1, 1, 4))
    x5 = jnp.stack(gather_halo(x))
    up5 = jnp.concatenate(gather_halo(up), axis=0)
    out, dq, q5, k, v, stats = run_query(bias, x5, w_qkv, cos5, sin5, up)
    stats5 = jnp.stack(gather_halo(stats))
    lse = stats5[:, :HEADS] + jnp.where(used_by, 0.0, FAR)[:, None, None]
    delta = stats5[:, HEADS:]
    lse = jnp.transpose(lse, (1, 0, 2)).reshape(HEADS, SLOTS * ROWS)
    delta = jnp.transpose(delta, (1, 0, 2)).reshape(HEADS, SLOTS * ROWS)
    dk, dv = run_key(lse, delta, q5, up5, k, v, cos5[0], sin5[0])
    dqkv = jnp.concatenate([dq, dk, dv], axis=1)
    d_other = lax.ppermute(dqkv, "lon", SWAP)
    grad_x = lax.dot_general(dqkv, w_qkv, (((1,), (1,)), ((), ())), preferred_element_type=F32).astype(BF)
    tokens = x5[:2].reshape(2 * ROWS, 16, 2, 32)
    x_rows = lax.dynamic_index_in_dim(tokens, core, axis=2, keepdims=False).reshape(2 * ROWS, 512).T
    partial = run_weight(x_rows, jnp.concatenate([dqkv, d_other], axis=0))
    grad_w = run_reduce(partial)
    return (out[None], grad_x[None], grad_w)


def solution(mesh):
    return jax.shard_map(
        per_device,
        mesh=mesh,
        in_specs=(
            P("dates", "lon", None),
            P(),
            P("dates", "lon", None),
            P("dates", "lon"),
            P("dates", None),
        ),
        out_specs=(P("dates", "lon", None), P("dates", "lon", None), P("dates", "lon")),
        check_vma=False,
    )
```

```python
import functools

import jax
import jax.numpy as jnp
from jax import lax
from jax.experimental import pallas as pl
from jax.experimental.pallas import tpu as pltpu
from jax.sharding import PartitionSpec as P

HEADS = 16
W_MAX = 2
INTERP = 0.25
BASE = 10000.0
FAR = 1e30
LOG2E = 1.4426950408889634
BF = jnp.bfloat16
F32 = jnp.float32
MESH = pl.DeviceIdType.MESH
N_LON = 16
ROWS = 256
GROUPS = 4
SLOTS = 5


def dot(a, b):
    return lax.dot_general(a, b, (((1,), (0,)), ((), ())), preferred_element_type=F32)


def dot_t(a, b):
    return lax.dot_general(a, b, (((1,), (1,)), ((), ())), preferred_element_type=F32)


def lanes(shape):
    return lax.broadcasted_iota(jnp.int32, shape, len(shape) - 1)


def perm_matrix():
    source = lax.broadcasted_iota(jnp.int32, (256, 256), 0)
    column = lax.broadcasted_iota(jnp.int32, (256, 256), 1)
    wanted = (column // 32 % 4) * 64 + (column // 128) * 32 + column % 32
    return jnp.where(source == wanted, 1.0, 0.0).astype(BF)


def turn(value, cosine, sine):
    a, c = value[:, :128], value[:, 128:]
    return jnp.concatenate([a * cosine - c * sine, a * sine + c * cosine], axis=1)


def turn_back(value, cosine, sine):
    a, c = value[:, :128], value[:, 128:]
    return jnp.concatenate([a * cosine + c * sine, c * cosine - a * sine], axis=1)


def query_kernel(bias_ref, x_hbm, w_hbm, up_hbm, spots_ref, freq_ref,
                 out_ref, dq_ref, q_ref, k_ref, v_ref, cos_ref, sin_ref, up_out, stats_out,
                 xs, spots, wbuf, wpair, up, kbuf, vbuf, cos5, sin5,
                 local, x_send, x_recv, p_send, p_recv, u_send, u_recv, s_send, s_recv):
    lon = lax.axis_index("lon")
    core = lax.rem(lon, 2)
    toward = 1 - 2 * core
    partner = {"lon": lon + toward}
    near_lon = lax.rem(lon - toward + N_LON, N_LON)
    near = {"lon": near_lon}
    ahead = {"lon": lax.rem(lon + 2 * toward + N_LON, N_LON)}
    behind = {"lon": lax.rem(lon - 2 * toward + N_LON, N_LON)}

    bring = [pltpu.make_async_copy(x_hbm, xs.at[0], local.at[0]),
             pltpu.make_async_copy(w_hbm, wbuf, local.at[1]),
             pltpu.make_async_copy(up_hbm, up, local.at[2])]
    for copy in bring:
        copy.start()
    barrier = pltpu.get_barrier_semaphore()
    for peer in (partner, near, ahead, behind):
        pl.semaphore_signal(barrier, inc=1, device_id=peer, device_id_type=MESH)
    pl.semaphore_wait(barrier, 4)

    def remote(source, target, send_sem, recv_sem, peer):
        return pltpu.make_async_remote_copy(src_ref=source, dst_ref=target, send_sem=send_sem, recv_sem=recv_sem,
                                            device_id=peer, device_id_type=MESH)

    routes = ((1, partner), (2, near), (3, ahead))
    p_copies = {slot: remote(spots_ref, spots.at[slot], p_send.at[slot], p_recv.at[slot], peer) for slot, peer in routes}
    p_copies[4] = remote(spots.at[2], spots.at[4], p_send.at[4], p_recv.at[4], partner)
    x_copies = {slot: remote(x_hbm, xs.at[slot], x_send.at[slot], x_recv.at[slot], peer) for slot, peer in routes}
    x_copies[4] = remote(xs.at[2], xs.at[4], x_send.at[4], x_recv.at[4], partner)

    def block(slot):
        return pl.ds(slot * ROWS, ROWS)

    u_copies = {slot: remote(up_hbm, up_out.at[block(slot)], u_send.at[slot], u_recv.at[slot], peer)
                for slot, peer in routes}
    u_copies[4] = remote(up_out.at[block(2)], up_out.at[block(4)], u_send.at[4], u_recv.at[4], partner)
    for slot in (2, 1, 3):
        p_copies[slot].start()
    x_copies[2].start()
    x_copies[1].start()

    perm = perm_matrix()
    bring[0].wait()
    bring[1].wait()

    @pl.loop(0, 2 * GROUPS)
    def _(g):
        cols = pl.ds(pl.multiple_of(g * 256, 256), 256)
        wpair[:, cols] = dot(wbuf[:, cols], perm).astype(BF)

    def tables(slot, row):
        spread = jnp.broadcast_to(row, (128, ROWS)).T
        angle = spread * freq_ref[0:1, :]
        cos5[slot] = jnp.cos(angle)
        sin5[slot] = jnp.sin(angle)

    def project(slot):
        @pl.loop(0, GROUPS)
        def _(g):
            def cols(part):
                return pl.ds(pl.multiple_of(g * 256 + part * 1024, 256), 256)

            x = xs[slot]
            cosine, sine = cos5[slot], sin5[slot]
            query = turn(dot(x, wpair[:, cols(0)]), cosine, sine).astype(BF).astype(F32) * 0.125
            q_ref[block(slot), cols(0)] = query.astype(BF)
            kbuf[block(slot), cols(0)] = turn(dot(x, wpair[:, cols(1)]), cosine, sine).astype(BF)
            vbuf[block(slot), cols(0)] = dot(x, wbuf[:, cols(2)]).astype(BF)

    tables(0, spots_ref[0:1, :])
    project(0)
    x_copies[2].wait_send()
    x_copies[3].start()
    p_copies[1].wait()
    x_copies[1].wait()
    tables(1, spots[1, 0:1, :])
    project(1)
    p_copies[2].wait()
    p_copies[4].start()
    x_copies[2].wait_recv()
    x_copies[4].start()
    tables(2, spots[2, 0:1, :])
    project(2)
    p_copies[3].wait()
    p_copies[4].wait()
    tables(3, spots[3, 0:1, :])
    tables(4, spots[4, 0:1, :])
    x_copies[4].wait()
    project(4)
    x_copies[3].wait()
    u_copies[2].start()
    u_copies[1].start()
    u_copies[3].start()
    bring[2].wait()
    keep_up = pltpu.make_async_copy(up, up_out.at[block(0)], local.at[3])
    keep_up.start()
    project(3)
    k_ref[...] = kbuf[block(0)]
    v_ref[...] = vbuf[block(0)]
    cos_ref[...] = cos5[0]
    sin_ref[...] = sin5[0]
    lane = lanes((ROWS, 256))
    lane_pair = lane // 32 % 4
    lane_flat = lane // 64
    stat_lane = lanes((ROWS, 128))
    zero = jnp.zeros((), BF)

    def s_copy(g, slot, peer):
        return remote(stats_out.at[2 if slot == 4 else 0, g], stats_out.at[slot, g],
                      s_send.at[slot, g], s_recv.at[slot, g], peer)

    @pl.loop(0, GROUPS)
    def _(g):
        cols = pl.ds(pl.multiple_of(g * 256, 256), 256)
        query = q_ref[block(0), cols]
        keys, values, up_g = kbuf[:, cols], vbuf[:, cols], up[:, cols]
        out = jnp.zeros((ROWS, 256), F32)
        dquery = jnp.zeros((ROWS, 256), F32)
        now = jnp.zeros((ROWS, 128), F32)
        for head in range(4):
            own_pair = lane_pair == head
            own_flat = lane_flat == head
            scores = dot_t(jnp.where(own_pair, query, zero), keys) * LOG2E
            row_max = None
            for slot in range(SLOTS):
                one = jnp.max(scores[:, slot * ROWS:(slot + 1) * ROWS], axis=1, keepdims=True) - bias_ref[0, slot]
                row_max = one if row_max is None else jnp.maximum(row_max, one)
            parts = []
            total = None
            for slot in range(SLOTS):
                one = jnp.exp2(scores[:, slot * ROWS:(slot + 1) * ROWS] - (row_max + bias_ref[0, slot]))
                part_sum = jnp.sum(one, axis=1, keepdims=True)
                total = part_sum if total is None else total + part_sum
                parts.append(one)
            weights = jnp.concatenate(parts, axis=1)
            inverse = 1.0 / total
            attended = dot(weights.astype(BF), values) * inverse
            attended = attended.astype(BF).astype(F32)
            out = jnp.where(own_flat, attended, out)
            up_own = jnp.where(own_flat, up_g, zero)
            delta = jnp.sum(up_own.astype(F32) * attended, axis=1, keepdims=True)
            dprobs = dot_t(up_own, values)
            dscores = (weights * (dprobs - delta)).astype(BF)
            dquery = jnp.where(own_pair, dot(dscores, keys) * (inverse * 0.125), dquery)
            now = jnp.where(stat_lane == head, row_max + jnp.log2(total), now)
            now = jnp.where(stat_lane == head + 4, delta, now)
        out_ref[:, cols] = out.astype(BF)
        dquery = turn_back(dquery, cos5[0], sin5[0]).astype(BF)
        dq_ref[:, cols] = dot_t(dquery, perm).astype(BF)
        stats_out[0, g] = now.T[:8]
        for slot, peer in routes:
            s_copy(g, slot, peer).start()

        @pl.when(g > 0)
        def _():
            s_copy(g - 1, 2, near).wait_recv()
            s_copy(g - 1, 4, partner).start()

    s_copy(GROUPS - 1, 2, near).wait_recv()
    s_copy(GROUPS - 1, 4, partner).start()
    u_copies[2].wait()
    u_copies[4].start()
    u_copies[1].wait()
    u_copies[3].wait()
    keep_up.wait()

    @pl.loop(0, GROUPS)
    def _(g):
        s_copy(g, 1, partner).wait()
        s_copy(g, 2, near).wait_send()
        s_copy(g, 3, ahead).wait()
        s_copy(g, 4, partner).wait()

    u_copies[4].wait()


def key_kernel(bias_ref, stats_ref, q_ref, up_ref, k_ref, v_ref, cos_ref, sin_ref, dk_ref, dv_ref):
    perm = perm_matrix()
    lane = lanes((ROWS, 256))
    lane_pair = lane // 32 % 4
    lane_flat = lane // 64
    zero = jnp.zeros((), BF)
    key, value = k_ref[...], v_ref[...]
    dkey = jnp.zeros((ROWS, 256), F32)
    dvalue = jnp.zeros((ROWS, 256), F32)
    for head in range(4):
        own_pair = lane_pair == head
        own_flat = lane_flat == head
        lse = jnp.concatenate([stats_ref[slot, 0, head:head + 1] + bias_ref[0, slot] for slot in range(SLOTS)], axis=1)
        delta = jnp.concatenate([stats_ref[slot, 0, head + 4:head + 5] for slot in range(SLOTS)], axis=1)
        scores = dot_t(jnp.where(own_pair, key, zero), q_ref[...]) * LOG2E
        probs = jnp.exp2(scores - lse)
        dprobs = dot_t(jnp.where(own_flat, value, zero), up_ref[...])
        dscores = (probs * (dprobs - delta)).astype(BF)
        dvalue = jnp.where(own_flat, dot(probs.astype(BF), up_ref[...]), dvalue)
        dkey = jnp.where(own_pair, dot(dscores, q_ref[...]), dkey)
    dkey = turn_back(dkey, cos_ref[...], sin_ref[...]).astype(BF)
    dk_ref[...] = dot_t(dkey, perm).astype(BF)
    dv_ref[...] = dvalue.astype(BF)


def run_query(bias, x, w, up, spots, freq):
    vmem = pl.BlockSpec(memory_space=pltpu.VMEM)
    hbm = pl.BlockSpec(memory_space=pl.ANY)
    dma = pltpu.SemaphoreType.DMA
    bf = lambda rows: jax.ShapeDtypeStruct((rows, 1024), BF)
    return pl.pallas_call(
        query_kernel,
        in_specs=[pl.BlockSpec(memory_space=pltpu.SMEM), hbm, hbm, hbm, vmem, vmem],
        out_specs=[vmem, vmem, vmem, vmem, vmem, vmem, vmem, hbm, vmem],
        out_shape=[bf(ROWS), bf(ROWS), bf(SLOTS * ROWS), bf(ROWS), bf(ROWS),
                   jax.ShapeDtypeStruct((ROWS, 128), F32), jax.ShapeDtypeStruct((ROWS, 128), F32),
                   bf(SLOTS * ROWS), jax.ShapeDtypeStruct((SLOTS, GROUPS, 8, ROWS), F32)],
        scratch_shapes=[
            pltpu.VMEM((SLOTS, ROWS, 1024), BF),
            pltpu.VMEM((SLOTS, 8, ROWS), F32),
            pltpu.VMEM((1024, 3072), BF),
            pltpu.VMEM((1024, 2048), BF),
            pltpu.VMEM((ROWS, 1024), BF),
            pltpu.VMEM((SLOTS * ROWS, 1024), BF),
            pltpu.VMEM((SLOTS * ROWS, 1024), BF),
            pltpu.VMEM((SLOTS, ROWS, 128), F32),
            pltpu.VMEM((SLOTS, ROWS, 128), F32),
            dma((4,)), dma((5,)), dma((5,)), dma((5,)), dma((5,)), dma((5,)), dma((5,)),
            dma((5, GROUPS)), dma((5, GROUPS)),
        ],
        compiler_params=pltpu.CompilerParams(collective_id=1, has_side_effects=True, vmem_limit_bytes=60 * 2**20),
        cost_estimate=pl.CostEstimate(flops=30 * 10**9, bytes_accessed=12 * 2**20, transcendentals=5 * 2**20),
        name="query_side",
    )(bias, x, w, up, spots, freq)


def run_key(bias, stats, q5, up5, k, v, cosine, sine):
    full = lambda *shape: pl.BlockSpec(shape, lambda g: (0,) * len(shape))
    col = lambda rows: pl.BlockSpec((rows, 256), lambda g: (0, g))
    bf = lambda rows: jax.ShapeDtypeStruct((rows, 1024), BF)
    return pl.pallas_call(
        key_kernel,
        grid=(GROUPS,),
        in_specs=[pl.BlockSpec(memory_space=pltpu.SMEM), pl.BlockSpec((SLOTS, 1, 8, ROWS), lambda g: (0, g, 0, 0)),
                  col(SLOTS * ROWS), col(SLOTS * ROWS),
                  col(ROWS), col(ROWS), full(ROWS, 128), full(ROWS, 128)],
        out_specs=[col(ROWS), col(ROWS)],
        out_shape=[bf(ROWS), bf(ROWS)],
        compiler_params=pltpu.CompilerParams(vmem_limit_bytes=60 * 2**20),
        cost_estimate=pl.CostEstimate(flops=12 * 10**9, bytes_accessed=8 * 2**20, transcendentals=5 * 2**20),
        name="key_side",
    )(bias, stats, q5, up5, k, v, cosine, sine)


def weight_kernel(x_ref, d_ref, g_ref):
    g_ref[0] = dot(x_ref[...], d_ref[...]).astype(BF)


def run_weight(x_rows, d_both):
    return pl.pallas_call(
        weight_kernel,
        grid=(8,),
        in_specs=[pl.BlockSpec((512, 512), lambda c: (0, 0)), pl.BlockSpec((512, 384), lambda c: (0, c))],
        out_specs=pl.BlockSpec((1, 512, 384), lambda c: (c, 0, 0)),
        out_shape=jax.ShapeDtypeStruct((8, 512, 384), BF),
        name="weight_partial",
    )(x_rows, d_both)


def reduce_kernel(g_ref, o_ref, in_x, in_y, sum_a, sum_b, in_a, in_b, sum_p, in_z, mine, theirs,
                  send_x, recv_x, send_y, recv_y, send_a, recv_a, send_b, recv_b, send_z, recv_z, send_c, recv_c):
    lon, dates = lax.axis_index("lon"), lax.axis_index("dates")
    x, y_lo, core = lon // 4, lon // 2 % 2, lon % 2
    z, y_hi = dates // 2, dates % 2
    y = y_hi * 2 + y_lo

    def at(px, py, pz, pc):
        return {"lon": px * 4 + py % 2 * 2 + pc, "dates": pz * 2 + py // 2}

    x_peers = [lax.rem(x + step, 4) for step in (1, 2, 3)]
    y_peers = [lax.rem(y + step, 4) for step in (1, 2, 3)]
    z_peers = [lax.rem(z + step, 8) for step in range(1, 8)]
    barrier = pltpu.get_barrier_semaphore()
    peers = [at(p, y, z, core) for p in x_peers] + [at(x, p, z, core) for p in y_peers]
    peers += [at(x, y, p, core) for p in z_peers] + [at(x, y, z, 1 - core)]
    for peer in peers:
        pl.semaphore_signal(barrier, inc=1, device_id=peer, device_id_type=MESH)
    pl.semaphore_wait(barrier, len(peers))

    def send(source, target, send_sem, recv_sem, peer):
        copy = pltpu.make_async_remote_copy(src_ref=source, dst_ref=target, send_sem=send_sem, recv_sem=recv_sem,
                                            device_id=peer, device_id_type=MESH)
        copy.start()
        return copy

    first_a = [send(g_ref.at[p, :, pl.ds(0, 4)], in_x.at[i], send_x.at[i], recv_x.at[i], at(p, y, z, core))
               for i, p in enumerate(x_peers)]
    first_b = [send(g_ref.at[:, p % 2, pl.ds(4, 4), p // 2], in_y.at[i], send_y.at[i], recv_y.at[i], at(x, p, z, core))
               for i, p in enumerate(y_peers)]
    for copy in first_a:
        copy.wait()
    for lo in range(2):
        for hi in range(2):
            total = g_ref[x, lo, 0:4, hi].astype(F32)
            for i in range(3):
                total += in_x[i, lo, :, hi].astype(F32)
            sum_a[hi, lo] = total.astype(BF)
    second_a = [send(sum_a.at[p // 2, p % 2], in_a.at[i], send_a.at[i], recv_a.at[i], at(x, p, z, core))
                for i, p in enumerate(y_peers)]
    for copy in first_b:
        copy.wait()
    for px in range(4):
        total = g_ref[px, y_lo, 4:8, y_hi].astype(F32)
        for i in range(3):
            total += in_y[i, px].astype(F32)
        sum_b[px] = total.astype(BF)
    second_b = [send(sum_b.at[p], in_b.at[i], send_b.at[i], recv_b.at[i], at(p, y, z, core))
                for i, p in enumerate(x_peers)]
    for copy in second_a:
        copy.wait()
    total = sum_a[y_hi, y_lo].astype(F32)
    for i in range(3):
        total += in_a[i].astype(F32)
    sum_p[0:4] = total.astype(BF)
    for copy in second_b:
        copy.wait()
    total = sum_b[x].astype(F32)
    for i in range(3):
        total += in_b[i].astype(F32)
    sum_p[4:8] = total.astype(BF)
    third = [send(sum_p.at[p], in_z.at[i], send_z.at[i], recv_z.at[i], at(x, y, p, core))
             for i, p in enumerate(z_peers)]
    for copy in third:
        copy.wait()
    total = sum_p[z].astype(F32)
    for i in range(7):
        total += in_z[i].astype(F32)
    total = total * (65536.0 ** -0.5)
    mine[0] = total[:, :192]
    mine[1] = total[:, 192:]
    last = send(mine.at[1 - core], theirs, send_c, recv_c, at(x, y, z, 1 - core))
    last.wait()
    own = mine[core]
    other = theirs[...]
    o_ref[pl.ds(pl.multiple_of(core * 32, 32), 32), :] = own
    o_ref[pl.ds(pl.multiple_of(32 - core * 32, 32), 32), :] = other


def run_reduce(partial):
    dma = pltpu.SemaphoreType.DMA
    return pl.pallas_call(
        reduce_kernel,
        in_specs=[pl.BlockSpec(memory_space=pltpu.VMEM)],
        out_specs=pl.BlockSpec(memory_space=pltpu.VMEM),
        out_shape=jax.ShapeDtypeStruct((64, 192), F32),
        scratch_shapes=[
            pltpu.VMEM((3, 2, 4, 2, 32, 384), BF),
            pltpu.VMEM((3, 4, 4, 32, 384), BF),
            pltpu.VMEM((2, 2, 4, 32, 384), BF),
            pltpu.VMEM((4, 4, 32, 384), BF),
            pltpu.VMEM((3, 4, 32, 384), BF),
            pltpu.VMEM((3, 4, 32, 384), BF),
            pltpu.VMEM((8, 32, 384), BF),
            pltpu.VMEM((7, 32, 384), BF),
            pltpu.VMEM((2, 32, 192), F32),
            pltpu.VMEM((32, 192), F32),
            dma((3,)), dma((3,)), dma((3,)), dma((3,)), dma((3,)), dma((3,)), dma((3,)), dma((3,)),
            dma((7,)), dma((7,)), dma, dma,
        ],
        compiler_params=pltpu.CompilerParams(collective_id=0, has_side_effects=True, vmem_limit_bytes=40 * 2**20),
        name="weight_reduce",
    )(partial.reshape(4, 2, 8, 2, 32, 384))


SWAP = [(i, i ^ 1) for i in range(N_LON)]


def per_device(features, w_qkv, grad_out, positions, block_list):
    x, up = features[0], grad_out[0]
    core = lax.axis_index("lon") % 2
    toward = 1 - 2 * core
    offsets = jnp.stack([jnp.int32(0), toward, -toward, -2 * toward, 2 * toward])
    listed = block_list[0]
    used = jnp.any(listed[None, :] == offsets[:, None], axis=1)
    used_by = jnp.any(listed[None, :] == -offsets[:, None], axis=1)
    bias = jnp.where(used, 0.0, FAR).astype(F32).reshape(1, SLOTS)
    bias_by = jnp.where(used_by, 0.0, FAR).astype(F32).reshape(1, SLOTS)
    pair_index = jnp.arange(32, dtype=F32)
    frequency = INTERP * BASE ** (-2.0 * pair_index / 64)
    freq = jnp.broadcast_to(jnp.tile(frequency, 4)[None], (8, 128))
    spots = jnp.broadcast_to(positions.astype(F32), (8, ROWS))
    out, dq, q5, k, v, cosine, sine, up5, stats = run_query(bias, x, w_qkv, up, spots, freq)
    dk, dv = run_key(bias_by, stats, q5, up5, k, v, cosine, sine)
    dqkv = jnp.concatenate([dq, dk, dv], axis=1)
    d_other = lax.ppermute(dqkv, "lon", SWAP)
    x_other = lax.ppermute(x, "lon", SWAP)
    grad_x = lax.dot_general(dqkv, w_qkv, (((1,), (1,)), ((), ())), preferred_element_type=F32).astype(BF)
    tokens = jnp.concatenate([x, x_other], axis=0).reshape(2 * ROWS, 16, 2, 32)
    x_rows = lax.dynamic_index_in_dim(tokens, core, axis=2, keepdims=False).reshape(2 * ROWS, 512).T
    partial = run_weight(x_rows, jnp.concatenate([dqkv, d_other], axis=0))
    grad_w = run_reduce(partial)
    return (out[None], grad_x[None], grad_w)


def solution(mesh):
    return jax.shard_map(
        per_device,
        mesh=mesh,
        in_specs=(
            P("dates", "lon", None),
            P(),
            P("dates", "lon", None),
            P("dates", "lon"),
            P("dates", None),
        ),
        out_specs=(P("dates", "lon", None), P("dates", "lon", None), P("dates", "lon")),
        check_vma=False,
    )
```

```python
import jax
import jax.numpy as jnp
from jax import lax
from jax.experimental import pallas as pl
from jax.experimental.pallas import tpu as pltpu
from jax.sharding import PartitionSpec as P

INTERP = 0.25
BASE = 10000.0
FAR = 1e30
LOG2E = 1.4426950408889634
BF = jnp.bfloat16
F32 = jnp.float32
MESH = pl.DeviceIdType.MESH
ROWS = 256
GROUPS = 4
SLOTS = 5
PIECES = 4


def dot(a, b):
    return lax.dot_general(a, b, (((1,), (0,)), ((), ())), preferred_element_type=F32)


def dot_t(a, b):
    return lax.dot_general(a, b, (((1,), (1,)), ((), ())), preferred_element_type=F32)


def lanes(shape):
    return lax.broadcasted_iota(jnp.int32, shape, len(shape) - 1)


def perm_matrix():
    source = lax.broadcasted_iota(jnp.int32, (256, 256), 0)
    column = lax.broadcasted_iota(jnp.int32, (256, 256), 1)
    wanted = (column // 32 % 4) * 64 + (column // 128) * 32 + column % 32
    return jnp.where(source == wanted, 1.0, 0.0).astype(BF)


def turn(value, cosine, sine):
    a, c = value[:, :128], value[:, 128:]
    return jnp.concatenate([a * cosine - c * sine, a * sine + c * cosine], axis=1)


def turn_back(value, cosine, sine):
    a, c = value[:, :128], value[:, 128:]
    return jnp.concatenate([a * cosine + c * sine, c * cosine - a * sine], axis=1)


def step_kernel(bias_ref, x_hbm, w_hbm, up_hbm, spots_ref, freq_ref,
                out_ref, gx_ref, gw_ref,
                perm_ref, xs, spots, wbuf, wpair, upbuf, qbuf, kbuf, vbuf, cos5, sin5, stats, both, xt,
                g_buf, in_x, in_y, sum_a, sum_b, in_a, in_b, sum_p, in_z, mine, theirs,
                local, x_send, x_recv, p_send, p_recv, u_send, u_recv, s_send, s_recv, d_send, d_recv,
                send_x, recv_x, send_y, recv_y, send_a, recv_a, send_b, recv_b, send_z, recv_z, send_c, recv_c):
    lon, dates = lax.axis_index("lon"), lax.axis_index("dates")
    x, y_lo, core = lon // 4, lax.rem(lon // 2, 2), lax.rem(lon, 2)
    z, y_hi = dates // 2, lax.rem(dates, 2)
    y = y_hi * 2 + y_lo
    step = 1 - 2 * y_lo

    def at(px, py, pz, pc):
        return {"lon": lax.rem(px + 4, 4) * 4 + lax.rem(py, 2) * 2 + pc, "dates": pz * 2 + py // 2}

    other_y = y_hi * 2 + 1 - y_lo
    partner = at(x, y, z, 1 - core)
    pair = at(x, other_y, z, core)
    onward = at(x + step, y, z, core)
    diagonal = at(x - step, other_y, z, core)
    passing = 2 + lax.rem(core + y_lo, 2)
    x_peers = [lax.rem(x + i, 4) for i in (1, 2, 3)]
    y_peers = [lax.rem(y + i, 4) for i in (1, 2, 3)]
    z_peers = [lax.rem(z + i, 8) for i in range(1, 8)]

    bring = [pltpu.make_async_copy(x_hbm, xs.at[0], local.at[0]),
             pltpu.make_async_copy(w_hbm, wbuf, local.at[1]),
             pltpu.make_async_copy(up_hbm, upbuf.at[pl.ds(0, ROWS)], local.at[2])]
    for copy in bring:
        copy.start()
    barrier = pltpu.get_barrier_semaphore()
    peers = [partner, diagonal] + [at(p, y, z, core) for p in x_peers] + [at(x, p, z, core) for p in y_peers]
    peers += [at(x, y, p, core) for p in z_peers]
    for peer in peers:
        pl.semaphore_signal(barrier, inc=1, device_id=peer, device_id_type=MESH)
    pl.semaphore_wait(barrier, len(peers))

    def remote(source, target, send_sem, recv_sem, peer):
        return pltpu.make_async_remote_copy(src_ref=source, dst_ref=target, send_sem=send_sem, recv_sem=recv_sem,
                                            device_id=peer, device_id_type=MESH)

    routes = ((1, partner), (2, pair), (3, diagonal))
    p_copies = {slot: remote(spots_ref, spots.at[slot], p_send.at[slot], p_recv.at[slot], peer) for slot, peer in routes}
    p_copies[4] = remote(spots.at[passing], spots.at[4], p_send.at[4], p_recv.at[4], partner)

    def piece(j):
        return pl.ds(j * (ROWS // PIECES), ROWS // PIECES)

    x_partner = remote(x_hbm, xs.at[1], x_send.at[0], x_recv.at[0], partner)
    x_pass = remote(xs.at[passing], xs.at[4], x_send.at[1], x_recv.at[1], partner)
    x_pair = [remote(x_hbm.at[piece(j)], xs.at[2, piece(j)], x_send.at[2 + j], x_recv.at[2 + j], pair)
              for j in range(PIECES)]
    x_cross = [remote(xs.at[2, piece(j)], xs.at[3, piece(j)], x_send.at[2 + PIECES + j], x_recv.at[2 + PIECES + j], onward)
               for j in range(PIECES)]

    def block(slot):
        return pl.ds(pl.multiple_of(slot * ROWS, ROWS), ROWS)

    u_copies = {slot: remote(up_hbm, upbuf.at[block(slot)], u_send.at[slot], u_recv.at[slot], peer)
                for slot, peer in routes[:2]}
    u_copies[3] = remote(upbuf.at[block(2)], upbuf.at[block(3)], u_send.at[3], u_recv.at[3], onward)
    u_copies[4] = remote(upbuf.at[block(passing)], upbuf.at[block(4)], u_send.at[4], u_recv.at[4], partner)
    for slot in (1, 2, 3):
        p_copies[slot].start()
    for copy in x_pair:
        copy.start()
    x_partner.start()
    u_copies[2].start()
    u_copies[1].start()

    perm_ref[...] = perm_matrix()
    bring[0].wait()
    bring[1].wait()

    def cols(part, g):
        return pl.ds(pl.multiple_of(part * 1024 + g * 256, 256), 256)

    @pl.loop(0, 2 * GROUPS)
    def _(g):
        wpair[:, cols(0, g)] = dot(wbuf[:, cols(0, g)], perm_ref[...]).astype(BF)

    def tables(slot, row):
        spread = jnp.broadcast_to(row, (128, ROWS)).T
        angle = spread * freq_ref[0:1, :]
        cos5[slot] = jnp.cos(angle)
        sin5[slot] = jnp.sin(angle)

    def project(slot):
        @pl.loop(0, GROUPS)
        def _(g):
            tokens = xs[slot]
            cosine, sine = cos5[slot], sin5[slot]
            query = turn(dot(tokens, wpair[:, cols(0, g)]), cosine, sine).astype(BF).astype(F32) * 0.125
            qbuf[block(slot), cols(0, g)] = query.astype(BF)
            kbuf[block(slot), cols(0, g)] = turn(dot(tokens, wpair[:, cols(1, g)]), cosine, sine).astype(BF)
            vbuf[block(slot), cols(0, g)] = dot(tokens, wbuf[:, cols(2, g)]).astype(BF)

    def hand_on(j):
        x_pair[j].wait_recv()
        x_cross[j].start()

    def stripes(slot):
        row = lax.broadcasted_iota(jnp.int32, (128, 256), 0)
        chosen = lanes((128, 256)) == row // 32 * 64 + core * 32 + row % 32
        select = jnp.where(chosen, 1.0, 0.0).astype(BF)
        for g in range(GROUPS):
            xt[g * 128:(g + 1) * 128, slot * ROWS:(slot + 1) * ROWS] = dot_t(select, xs[slot, :, g * 256:(g + 1) * 256]).astype(BF)

    hand_on(0)
    tables(0, spots_ref[0:1, :])
    project(0)
    hand_on(1)
    p_copies[1].wait()
    tables(1, spots[1, 0:1, :])
    x_partner.wait()
    project(1)
    hand_on(2)
    p_copies[2].wait()
    p_copies[3].wait()
    p_copies[4].start()
    tables(2, spots[2, 0:1, :])
    tables(3, spots[3, 0:1, :])
    hand_on(3)
    project(2)
    p_copies[4].wait()
    tables(4, spots[4, 0:1, :])
    stripes(0)
    stripes(1)
    for copy in x_cross:
        copy.wait()
    x_pass.start()
    project(3)
    for copy in x_pair:
        copy.wait_send()
    bring[2].wait()
    x_pass.wait()
    project(4)
    lane = lanes((ROWS, 256))
    lane_pair = lane // 32 % 4
    lane_flat = lane // 64
    stat_lane = lanes((ROWS, 128))
    zero = jnp.zeros((), BF)

    def s_copy(g, slot, peer):
        return remote(stats.at[passing if slot == 4 else 0, g], stats.at[slot, g],
                      s_send.at[slot, g], s_recv.at[slot, g], peer)

    def d_copy(part, g):
        return remote(both.at[pl.ds(0, ROWS), cols(part, g)], both.at[pl.ds(ROWS, ROWS), cols(part, g)],
                      d_send.at[part, g], d_recv.at[part, g], partner)

    @pl.loop(0, GROUPS)
    def _(g):
        mid = cols(0, g)
        query = qbuf[block(0), mid]
        up_g = upbuf[block(0), mid]
        out = jnp.zeros((ROWS, 256), F32)
        dquery = jnp.zeros((ROWS, 256), F32)
        now = jnp.zeros((ROWS, 128), F32)
        for head in range(4):
            own_pair = lane_pair == head
            own_flat = lane_flat == head
            scores = dot_t(jnp.where(own_pair, query, zero), kbuf[:, mid]) * LOG2E
            row_max = None
            for slot in range(SLOTS):
                one = jnp.max(scores[:, slot * ROWS:(slot + 1) * ROWS], axis=1, keepdims=True) - bias_ref[0, slot]
                row_max = one if row_max is None else jnp.maximum(row_max, one)
            parts = []
            total = None
            for slot in range(SLOTS):
                one = jnp.exp2(scores[:, slot * ROWS:(slot + 1) * ROWS] - (row_max + bias_ref[0, slot]))
                part_sum = jnp.sum(one, axis=1, keepdims=True)
                total = part_sum if total is None else total + part_sum
                parts.append(one)
            weights = jnp.concatenate(parts, axis=1)
            inverse = 1.0 / total
            attended = dot(weights.astype(BF), vbuf[:, mid]) * inverse
            attended = attended.astype(BF).astype(F32)
            out = jnp.where(own_flat, attended, out)
            up_own = jnp.where(own_flat, up_g, zero)
            delta = jnp.sum(up_own.astype(F32) * attended, axis=1, keepdims=True)
            dprobs = dot_t(up_own, vbuf[:, mid])
            dscores = (weights * (dprobs - delta)).astype(BF)
            dquery = jnp.where(own_pair, dot(dscores, kbuf[:, mid]) * (inverse * 0.125), dquery)
            now = jnp.where(stat_lane == head, row_max + jnp.log2(total), now)
            now = jnp.where(stat_lane == head + 4, delta, now)
        stats[0, g] = now.T[:8]
        dquery = turn_back(dquery, cos5[0], sin5[0]).astype(BF)
        both[0:ROWS, mid] = dot_t(dquery, perm_ref[...]).astype(BF)
        out_ref[:, mid] = out.astype(BF)
        for slot, peer in routes:
            s_copy(g, slot, peer).start()
        d_copy(0, g).start()

        def pass_stats(g):
            s_copy(g, 2, pair).wait_recv()
            s_copy(g, 3, diagonal).wait_recv()
            s_copy(g, 4, partner).start()

        @pl.when(g > 0)
        def _():
            pass_stats(g - 1)

        @pl.when(g == 0)
        def _():
            u_copies[2].wait_recv()
            u_copies[3].start()

        @pl.when(g == 2)
        def _():
            u_copies[3].wait_recv()
            u_copies[4].start()

        @pl.when(g == GROUPS - 1)
        def _():
            pass_stats(g)

    def send_first(s):
        px, lo = s // 6, lax.rem(s // 3, 2)

        @pl.when(px != x)
        def _():
            slot = lax.rem(px - x + 3, 4)
            remote(g_buf.at[s, pl.ds(0, 4)], in_x.at[slot, s - 6 * px], send_x.at[slot], recv_x.at[slot],
                   at(px, y, z, core)).start()

        for hi in range(2):
            py = hi * 2 + lo

            @pl.when(py != y)
            def _():
                slot = lax.rem(py - y + 3, 4)
                remote(g_buf.at[s, pl.ds(4, 4), hi], in_y.at[slot, px * 3 + lax.rem(s, 3)], send_y.at[slot],
                       recv_y.at[slot], at(x, py, z, core)).start()

    def weight_piece(part, g):
        d_copy(part, g).wait_recv()
        value = dot(xt[...], both[:, cols(part, g)]).astype(BF)
        first = part * 8 + g * 2
        g_buf[first] = value[:, :128].reshape(8, 2, 32, 128)
        g_buf[first + 1] = value[:, 128:].reshape(8, 2, 32, 128)
        send_first(first)
        send_first(first + 1)

    @pl.loop(0, GROUPS)
    def _(g):
        mid = cols(0, g)
        s_copy(g, 1, partner).wait_recv()
        s_copy(g, 4, partner).wait_recv()

        @pl.when(g == 0)
        def _():
            u_copies[1].wait_recv()
            u_copies[4].wait_recv()

        weight_piece(0, g)
        key, value = kbuf[block(0), mid], vbuf[block(0), mid]
        dkey = jnp.zeros((ROWS, 256), F32)
        dvalue = jnp.zeros((ROWS, 256), F32)
        for head in range(4):
            own_pair = lane_pair == head
            own_flat = lane_flat == head
            lse = jnp.concatenate([stats[slot, g, head:head + 1] + bias_ref[1, slot] for slot in range(SLOTS)], axis=1)
            delta = jnp.concatenate([stats[slot, g, head + 4:head + 5] for slot in range(SLOTS)], axis=1)
            scores = dot_t(jnp.where(own_pair, key, zero), qbuf[:, mid]) * LOG2E
            probs = jnp.exp2(scores - lse)
            dprobs = dot_t(jnp.where(own_flat, value, zero), upbuf[:, mid])
            dscores = (probs * (dprobs - delta)).astype(BF)
            dvalue = jnp.where(own_flat, dot(probs.astype(BF), upbuf[:, mid]), dvalue)
            dkey = jnp.where(own_pair, dot(dscores, qbuf[:, mid]), dkey)
        dkey = turn_back(dkey, cos5[0], sin5[0]).astype(BF)
        both[0:ROWS, cols(2, g)] = dvalue.astype(BF)
        both[0:ROWS, cols(1, g)] = dot_t(dkey, perm_ref[...]).astype(BF)
        d_copy(2, g).start()
        d_copy(1, g).start()

        @pl.when(g > 0)
        def _():
            weight_piece(2, g - 1)
            weight_piece(1, g - 1)

    weight_piece(2, GROUPS - 1)
    weight_piece(1, GROUPS - 1)

    def grad_x(j):
        rows = slice(j * 256, (j + 1) * 256)
        gx_ref[:, rows] = dot_t(both[0:ROWS], wbuf[rows]).astype(BF)

    grad_x(0)
    grad_x(1)
    first_a = [remote(in_x.at[i], in_x.at[i], send_x.at[i], recv_x.at[i], at(p, y, z, core)) for i, p in enumerate(x_peers)]
    first_b = [remote(in_y.at[i], in_y.at[i], send_y.at[i], recv_y.at[i], at(x, p, z, core)) for i, p in enumerate(y_peers)]
    for copy in first_a:
        copy.wait_recv()
    for j in range(6):
        total = g_buf[6 * x + j, 0:4].astype(F32)
        for i in range(3):
            total += in_x[i, j].astype(F32)
        sum_a[j] = total.astype(BF)
    second_a = [remote(sum_a.at[pl.ds(lax.rem(p, 2) * 3, 3), :, p // 2], in_a.at[i], send_a.at[i], recv_a.at[i],
                       at(x, p, z, core)) for i, p in enumerate(y_peers)]
    for copy in second_a:
        copy.start()
    for copy in first_b:
        copy.wait_recv()
    for px in range(4):
        for j in range(3):
            total = g_buf[px * 6 + y_lo * 3 + j, 4:8, y_hi].astype(F32)
            for i in range(3):
                total += in_y[i, px * 3 + j].astype(F32)
            sum_b[px * 3 + j] = total.astype(BF)
    second_b = [remote(sum_b.at[pl.ds(p * 3, 3)], in_b.at[i], send_b.at[i], recv_b.at[i], at(p, y, z, core))
                for i, p in enumerate(x_peers)]
    for copy in second_b:
        copy.start()
    grad_x(2)
    for copy in second_a:
        copy.wait_recv()
    for j in range(3):
        total = sum_a[y_lo * 3 + j, :, y_hi].astype(F32)
        for i in range(3):
            total += in_a[i, j].astype(F32)
        sum_p[0:4, j] = total.astype(BF)
    for copy in second_b:
        copy.wait_recv()
    for j in range(3):
        total = sum_b[x * 3 + j].astype(F32)
        for i in range(3):
            total += in_b[i, j].astype(F32)
        sum_p[4:8, j] = total.astype(BF)
    third = [remote(sum_p.at[p], in_z.at[i], send_z.at[i], recv_z.at[i], at(x, y, p, core)) for i, p in enumerate(z_peers)]
    for copy in third:
        copy.start()
    grad_x(3)
    for copy in first_a + first_b + second_a + second_b:
        copy.wait_send()
    u_copies[1].wait_send()
    u_copies[2].wait_send()
    u_copies[3].wait_send()
    u_copies[4].wait_send()

    @pl.loop(0, GROUPS)
    def _(g):
        for part in range(3):
            d_copy(part, g).wait_send()
        s_copy(g, 1, partner).wait_send()
        s_copy(g, 2, pair).wait_send()
        s_copy(g, 3, diagonal).wait_send()
        s_copy(g, 4, partner).wait_send()

    for copy in third:
        copy.wait()
    pieces = []
    for j in range(3):
        total = sum_p[z, j].astype(F32)
        for i in range(7):
            total += in_z[i, j].astype(F32)
        pieces.append(total * (65536.0 ** -0.5))
    total = jnp.concatenate(pieces, axis=1)
    mine[0] = total[:, :192]
    mine[1] = total[:, 192:]
    last = remote(mine.at[1 - core], theirs, send_c, recv_c, partner)
    last.start()
    gw_ref[pl.ds(pl.multiple_of(core * 32, 32), 32), :] = mine[core]
    last.wait()
    gw_ref[pl.ds(pl.multiple_of(32 - core * 32, 32), 32), :] = theirs[...]


def run_step(bias, x, w, up, spots, freq):
    vmem = pl.BlockSpec(memory_space=pltpu.VMEM)
    hbm = pl.BlockSpec(memory_space=pl.ANY)
    dma = pltpu.SemaphoreType.DMA
    block = jax.ShapeDtypeStruct((ROWS, 1024), BF)
    buffers = [
        ((256, 256), BF), ((SLOTS, ROWS, 1024), BF), ((SLOTS, 8, ROWS), F32), ((1024, 3072), BF), ((1024, 2048), BF),
        ((SLOTS * ROWS, 1024), BF), ((SLOTS * ROWS, 1024), BF), ((SLOTS * ROWS, 1024), BF), ((SLOTS * ROWS, 1024), BF),
        ((SLOTS, ROWS, 128), F32), ((SLOTS, ROWS, 128), F32), ((SLOTS, GROUPS, 8, ROWS), F32),
        ((2 * ROWS, 3072), BF), ((512, 512), BF),
        ((24, 8, 2, 32, 128), BF), ((3, 6, 4, 2, 32, 128), BF), ((3, 12, 4, 32, 128), BF), ((6, 4, 2, 32, 128), BF),
        ((12, 4, 32, 128), BF), ((3, 3, 4, 32, 128), BF), ((3, 3, 4, 32, 128), BF), ((8, 3, 32, 128), BF),
        ((7, 3, 32, 128), BF), ((2, 32, 192), F32), ((32, 192), F32),
    ]
    moves = (2 + 2 * PIECES,)
    semaphores = [dma((3,)), dma(moves), dma(moves)] + [dma((5,))] * 4 + [dma((5, GROUPS))] * 2 + [dma((3, GROUPS))] * 2
    semaphores += [dma((3,))] * 8 + [dma((7,))] * 2 + [dma, dma]
    return pl.pallas_call(
        step_kernel,
        in_specs=[pl.BlockSpec(memory_space=pltpu.SMEM), hbm, hbm, hbm, vmem, vmem],
        out_specs=[vmem, vmem, vmem],
        out_shape=[block, block, jax.ShapeDtypeStruct((64, 192), F32)],
        scratch_shapes=[pltpu.VMEM(shape, kind) for shape, kind in buffers] + semaphores,
        compiler_params=pltpu.CompilerParams(collective_id=0, has_side_effects=True, vmem_limit_bytes=63 * 2**20),
        name="whole_step",
    )(bias, x, w, up, spots, freq)


def per_device(features, w_qkv, grad_out, positions, block_list):
    lon = lax.axis_index("lon")
    toward, step = 1 - 2 * (lon % 2), 1 - 2 * (lon // 2 % 2)
    offsets = jnp.stack([jnp.int32(0), toward, 2 * step, -2 * step, -toward])
    sides = jnp.stack([offsets, -offsets])
    used = jnp.any(block_list[0][None, None, :] == sides[:, :, None], axis=2)
    bias = jnp.where(used, 0.0, FAR).astype(F32)
    pair_index = jnp.arange(32, dtype=F32)
    frequency = INTERP * BASE ** (-2.0 * pair_index / 64)
    freq = jnp.broadcast_to(jnp.tile(frequency, 4)[None], (8, 128))
    spots = jnp.broadcast_to(positions.astype(F32), (8, ROWS))
    out, grad_x, grad_w = run_step(bias, features[0], w_qkv, grad_out[0], spots, freq)
    return (out[None], grad_x[None], grad_w)


def solution(mesh):
    return jax.shard_map(
        per_device,
        mesh=mesh,
        in_specs=(
            P("dates", "lon", None),
            P(),
            P("dates", "lon", None),
            P("dates", "lon"),
            P("dates", None),
        ),
        out_specs=(P("dates", "lon", None), P("dates", "lon", None), P("dates", "lon")),
        check_vma=False,
    )
```

```python
import jax
import jax.numpy as jnp
import numpy as np
from jax import lax
from jax.experimental import pallas as pl
from jax.experimental.pallas import tpu as pltpu
from jax.sharding import PartitionSpec as P

INTERP = 0.25
BASE = 10000.0
FAR = 1e30
LOG2E = 1.4426950408889634
BF = jnp.bfloat16
F32 = jnp.float32
MESH = pl.DeviceIdType.MESH
ROWS = 256
GROUPS = 4
SLOTS = 5
PIECES = 4


def dot(a, b):
    return lax.dot_general(a, b, (((1,), (0,)), ((), ())), preferred_element_type=F32)


def dot_t(a, b):
    return lax.dot_general(a, b, (((1,), (1,)), ((), ())), preferred_element_type=F32)


def lanes(shape):
    return lax.broadcasted_iota(jnp.int32, shape, len(shape) - 1)


def perm_matrix():
    source = lax.broadcasted_iota(jnp.int32, (256, 256), 0)
    column = lax.broadcasted_iota(jnp.int32, (256, 256), 1)
    wanted = (column // 32 % 4) * 64 + (column // 128) * 32 + column % 32
    return jnp.where(source == wanted, 1.0, 0.0).astype(BF)


def turn(value, cosine, sine):
    a, c = value[:, :128], value[:, 128:]
    return jnp.concatenate([a * cosine - c * sine, a * sine + c * cosine], axis=1)


def turn_back(value, cosine, sine):
    a, c = value[:, :128], value[:, 128:]
    return jnp.concatenate([a * cosine + c * sine, c * cosine - a * sine], axis=1)


def step_kernel(list_ref, x_hbm, w_hbm, up_hbm, spots_ref, freq_ref,
                out_hbm, gx_hbm, gw_ref,
                out_ref, gx_ref,
                perm_ref, xs, spots, wbuf, wpair, upbuf, qbuf, kbuf, vbuf, cos5, sin5, stats, both, xt,
                g_buf, in_x, in_y, sum_a, sum_b, in_a, in_b, sum_p, in_z,
                local, x_send, x_recv, p_send, p_recv, u_send, u_recv, s_send, s_recv, d_send, d_recv,
                send_x, recv_x, send_y, recv_y, send_a, recv_a, send_b, recv_b, send_z, recv_z):
    lon, dates = lax.axis_index("lon"), lax.axis_index("dates")
    x, y_lo, core = lon // 4, lax.rem(lon // 2, 2), lax.rem(lon, 2)
    z, y_hi = dates // 2, lax.rem(dates, 2)
    y = y_hi * 2 + y_lo
    step = 1 - 2 * y_lo

    def at(px, py, pz, pc):
        return {"lon": lax.rem(px + 4, 4) * 4 + lax.rem(py, 2) * 2 + pc, "dates": pz * 2 + py // 2}

    other_y = y_hi * 2 + 1 - y_lo
    partner = at(x, y, z, 1 - core)
    pair = at(x, other_y, z, core)
    onward = at(x + step, y, z, core)
    diagonal = at(x - step, other_y, z, core)
    passing = 2 + lax.rem(core + y_lo, 2)
    x_peers = [lax.rem(x + i, 4) for i in (1, 2, 3)]
    y_peers = [lax.rem(y + i, 4) for i in (1, 2, 3)]
    z_peers = [lax.rem(z + i, 8) for i in range(1, 8)]

    bring = [pltpu.make_async_copy(x_hbm, xs.at[0], local.at[0]),
             pltpu.make_async_copy(w_hbm, wbuf, local.at[1]),
             pltpu.make_async_copy(up_hbm, upbuf.at[pl.ds(0, ROWS)], local.at[2])]
    for copy in bring:
        copy.start()
    barrier = pltpu.get_barrier_semaphore()
    peers = [partner, diagonal] + [at(p, y, z, core) for p in x_peers] + [at(x, p, z, core) for p in y_peers]
    peers += [at(x, y, p, c) for p in z_peers for c in range(2)]
    for peer in peers:
        pl.semaphore_signal(barrier, inc=1, device_id=peer, device_id_type=MESH)
    pl.semaphore_wait(barrier, len(peers))

    offsets = (0, 1 - 2 * core, 2 * step, -2 * step, 2 * core - 1)

    def bias(offset):
        found = list_ref[0, 0] == offset
        for i in range(1, 5):
            found = jnp.logical_or(found, list_ref[0, i] == offset)
        return jnp.where(found, 0.0, FAR)

    bias_to = [bias(offset) for offset in offsets]
    bias_from = [bias(-offset) for offset in offsets]

    def remote(source, target, send_sem, recv_sem, peer):
        return pltpu.make_async_remote_copy(src_ref=source, dst_ref=target, send_sem=send_sem, recv_sem=recv_sem,
                                            device_id=peer, device_id_type=MESH)

    routes = ((1, partner), (2, pair), (3, diagonal))
    p_copies = {slot: remote(spots_ref, spots.at[slot], p_send.at[slot], p_recv.at[slot], peer) for slot, peer in routes}
    p_copies[4] = remote(spots.at[passing], spots.at[4], p_send.at[4], p_recv.at[4], partner)

    def piece(j):
        return pl.ds(j * (ROWS // PIECES), ROWS // PIECES)

    x_partner = remote(x_hbm, xs.at[1], x_send.at[0], x_recv.at[0], partner)
    x_pair = [remote(x_hbm.at[piece(j)], xs.at[2, piece(j)], x_send.at[2 + j], x_recv.at[2 + j], pair)
              for j in range(PIECES)]
    x_cross = [remote(xs.at[2, piece(j)], xs.at[3, piece(j)], x_send.at[2 + PIECES + j], x_recv.at[2 + PIECES + j], onward)
               for j in range(PIECES)]
    x_pass = [remote(xs.at[passing, piece(j)], xs.at[4, piece(j)], x_send.at[2 + 2 * PIECES + j],
                     x_recv.at[2 + 2 * PIECES + j], partner) for j in range(PIECES)]

    def block(slot):
        return pl.ds(pl.multiple_of(slot * ROWS, ROWS), ROWS)

    def block_piece(slot, j):
        return pl.ds(slot * ROWS + j * (ROWS // PIECES), ROWS // PIECES)

    u_partner = remote(up_hbm, upbuf.at[block(1)], u_send.at[0], u_recv.at[0], partner)
    u_pass = remote(upbuf.at[block(passing)], upbuf.at[block(4)], u_send.at[1], u_recv.at[1], partner)
    u_pair = [remote(up_hbm.at[piece(j)], upbuf.at[block_piece(2, j)], u_send.at[2 + j], u_recv.at[2 + j], pair)
              for j in range(PIECES)]
    u_cross = [remote(upbuf.at[block_piece(2, j)], upbuf.at[block_piece(3, j)], u_send.at[2 + PIECES + j],
                      u_recv.at[2 + PIECES + j], onward) for j in range(PIECES)]
    for slot in (1, 2, 3):
        p_copies[slot].start()
    for copy in x_pair:
        copy.start()
    x_partner.start()
    for copy in u_pair:
        copy.start()
    u_partner.start()

    perm_ref[...] = perm_matrix()
    bring[0].wait()
    bring[1].wait()

    def cols(part, g):
        return pl.ds(pl.multiple_of(part * 1024 + g * 256, 256), 256)

    @pl.loop(0, 2 * GROUPS)
    def _(g):
        wpair[:, cols(0, g)] = dot(wbuf[:, cols(0, g)], perm_ref[...]).astype(BF)

    def tables(slot, row):
        spread = jnp.broadcast_to(row.astype(F32), (128, ROWS)).T
        angle = spread * freq_ref[0:1, :]
        cos5[slot] = jnp.cos(angle)
        sin5[slot] = jnp.sin(angle)

    def project(slot):
        into = block(slot)

        @pl.loop(0, GROUPS)
        def _(g):
            tokens = xs[slot]
            cosine, sine = cos5[slot], sin5[slot]
            query = turn(dot(tokens, wpair[:, cols(0, g)]), cosine, sine).astype(BF).astype(F32) * 0.125
            qbuf[into, cols(0, g)] = query.astype(BF)
            kbuf[into, cols(0, g)] = turn(dot(tokens, wpair[:, cols(1, g)]), cosine, sine).astype(BF)
            vbuf[into, cols(0, g)] = dot(tokens, wbuf[:, cols(2, g)]).astype(BF)

    def hand_on(j):
        x_pair[j].wait_recv()
        x_cross[j].start()

    def stripes(slot):
        row = lax.broadcasted_iota(jnp.int32, (128, 256), 0)
        chosen = lanes((128, 256)) == row // 32 * 64 + core * 32 + row % 32
        select = jnp.where(chosen, 1.0, 0.0).astype(BF)
        for g in range(GROUPS):
            xt[g * 128:(g + 1) * 128, slot * ROWS:(slot + 1) * ROWS] = dot_t(select, xs[slot, :, g * 256:(g + 1) * 256]).astype(BF)

    def hand_on_up(j):
        u_pair[j].wait_recv()
        u_cross[j].start()

    tables(0, spots_ref[...])
    hand_on(0)
    project(0)
    hand_on(1)
    p_copies[1].wait()
    tables(1, spots[1])
    x_partner.wait()
    project(1)
    hand_on(2)
    p_copies[2].wait()
    p_copies[3].wait()
    p_copies[4].start()
    tables(2, spots[2])
    tables(3, spots[3])
    hand_on(3)
    project(2)
    p_copies[4].wait()
    tables(4, spots[4])
    stripes(0)
    stripes(1)
    for cross, passed in zip(x_cross, x_pass):
        cross.wait_recv()
        passed.start()
    project(3)
    hand_on_up(0)
    bring[2].wait()
    for copy in x_pass:
        copy.wait_recv()
    project(4)
    hand_on_up(1)
    lane = lanes((ROWS, 256))
    lane_pair = lane // 32 % 4
    lane_flat = lane // 64
    stat_lane = lanes((ROWS, 128))
    zero = jnp.zeros((), BF)

    def s_copy(g, slot, peer):
        return remote(stats.at[passing if slot == 4 else 0, g], stats.at[slot, g],
                      s_send.at[slot, g], s_recv.at[slot, g], peer)

    def d_copy(part, g):
        return remote(both.at[pl.ds(0, ROWS), cols(part, g)], both.at[pl.ds(ROWS, ROWS), cols(part, g)],
                      d_send.at[part, g], d_recv.at[part, g], partner)

    def send_first(s):
        px, lo = s // 6, lax.rem(s // 3, 2)

        @pl.when(px != x)
        def _():
            slot = lax.rem(px - x + 3, 4)
            remote(g_buf.at[s, pl.ds(0, 4)], in_x.at[slot, s - 6 * px], send_x.at[slot], recv_x.at[slot],
                   at(px, y, z, core)).start()

        for hi in range(2):
            py = hi * 2 + lo

            @pl.when(py != y)
            def _():
                slot = lax.rem(py - y + 3, 4)
                remote(g_buf.at[s, pl.ds(4, 4), hi], in_y.at[slot, px * 3 + lax.rem(s, 3)], send_y.at[slot],
                       recv_y.at[slot], at(x, py, z, core)).start()

    def weight_piece(part, g):
        d_copy(part, g).wait_recv()
        value = dot(xt[...], both[:, cols(part, g)]).astype(BF)
        first = part * 8 + g * 2
        g_buf[first] = value[:, :128].reshape(8, 2, 32, 128)
        g_buf[first + 1] = value[:, 128:].reshape(8, 2, 32, 128)
        send_first(first)
        send_first(first + 1)

    def pass_stats(g):
        s_copy(g, 2, pair).wait_recv()
        s_copy(g, 3, diagonal).wait_recv()
        s_copy(g, 4, partner).start()

    def out_copy(g):
        return pltpu.make_async_copy(out_ref.at[:, cols(0, g)], out_hbm.at[:, cols(0, g)], local.at[3 + g])

    @pl.loop(0, GROUPS)
    def _(g):
        mid = cols(0, g)
        query = qbuf[block(0), mid]
        up_g = upbuf[block(0), mid]
        out = jnp.zeros((ROWS, 256), F32)
        dquery = jnp.zeros((ROWS, 256), F32)
        now = jnp.zeros((ROWS, 128), F32)
        for head in range(4):
            own_pair = lane_pair == head
            own_flat = lane_flat == head
            scores = dot_t(jnp.where(own_pair, query, zero), kbuf[:, mid])
            row_max = None
            for slot in range(SLOTS):
                left = slot * ROWS
                one = jnp.maximum(scores[:, left:left + 128], scores[:, left + 128:left + 256]) - bias_to[slot]
                row_max = one if row_max is None else jnp.maximum(row_max, one)
            row_max = jnp.max(row_max, axis=1, keepdims=True)
            parts = []
            total = None
            for slot in range(SLOTS):
                one = jnp.exp2((scores[:, slot * ROWS:(slot + 1) * ROWS] - (row_max + bias_to[slot])) * LOG2E)
                part_sum = one[:, :128] + one[:, 128:]
                total = part_sum if total is None else total + part_sum
                parts.append(one)
            total = jnp.sum(total, axis=1, keepdims=True)
            weights = jnp.concatenate(parts, axis=1)
            inverse = 1.0 / total
            attended = dot(weights.astype(BF), vbuf[:, mid]) * inverse
            attended = attended.astype(BF).astype(F32)
            out = jnp.where(own_flat, attended, out)
            up_own = jnp.where(own_flat, up_g, zero)
            delta = jnp.sum(up_own.astype(F32) * attended, axis=1, keepdims=True)
            dprobs = dot_t(up_own, vbuf[:, mid])
            dscores = (weights * (dprobs - delta)).astype(BF)
            dquery = jnp.where(own_pair, dot(dscores, kbuf[:, mid]) * (inverse * 0.125), dquery)
            now = jnp.where(stat_lane == head, row_max * LOG2E + jnp.log2(total), now)
            now = jnp.where(stat_lane == head + 4, delta, now)
        stats[0, g] = now.T[:8]
        dquery = turn_back(dquery, cos5[0], sin5[0]).astype(BF)
        both[0:ROWS, mid] = dot_t(dquery, perm_ref[...]).astype(BF)
        out_ref[:, mid] = out.astype(BF)
        for slot, peer in routes:
            s_copy(g, slot, peer).start()
        d_copy(0, g).start()
        out_copy(g).start()

        @pl.when(g == 0)
        def _():
            hand_on_up(2)
            hand_on_up(3)

        @pl.when(g == 2)
        def _():
            for copy in u_cross:
                copy.wait_recv()
            u_pass.start()

        @pl.when(g > 0)
        def _():
            pass_stats(g - 1)
            weight_piece(0, g - 1)

    def gx_copy(j):
        return pltpu.make_async_copy(gx_ref.at[:, pl.ds(j * 256, 256)], gx_hbm.at[:, pl.ds(j * 256, 256)], local.at[7 + j])

    def grad_x(j):
        rows = slice(j * 256, (j + 1) * 256)
        gx_ref[:, rows] = dot_t(both[0:ROWS], wbuf[rows]).astype(BF)
        gx_copy(j).start()

    @pl.loop(0, GROUPS)
    def _(g):
        mid = cols(0, g)
        s_copy(g, 1, partner).wait_recv()
        s_copy(g, 4, partner).wait_recv()

        @pl.when(g == 0)
        def _():
            u_partner.wait_recv()
            u_pass.wait_recv()

        key, value = kbuf[block(0), mid], vbuf[block(0), mid]
        dkey = jnp.zeros((ROWS, 256), F32)
        dvalue = jnp.zeros((ROWS, 256), F32)
        for head in range(4):
            own_pair = lane_pair == head
            own_flat = lane_flat == head
            lse = jnp.concatenate([stats[slot, g, head:head + 1] + bias_from[slot] for slot in range(SLOTS)], axis=1)
            delta = jnp.concatenate([stats[slot, g, head + 4:head + 5] for slot in range(SLOTS)], axis=1)
            scores = dot_t(jnp.where(own_pair, key, zero), qbuf[:, mid]) * LOG2E
            probs = jnp.exp2(scores - lse)
            dprobs = dot_t(jnp.where(own_flat, value, zero), upbuf[:, mid])
            dscores = (probs * (dprobs - delta)).astype(BF)
            dvalue = jnp.where(own_flat, dot(probs.astype(BF), upbuf[:, mid]), dvalue)
            dkey = jnp.where(own_pair, dot(dscores, qbuf[:, mid]), dkey)
            if head == 2:
                @pl.when(g == 0)
                def _():
                    pass_stats(GROUPS - 1)
                    weight_piece(0, GROUPS - 1)

                @pl.when(g > 0)
                def _():
                    weight_piece(2, g - 1)
                    weight_piece(1, g - 1)
        dkey = turn_back(dkey, cos5[0], sin5[0]).astype(BF)
        both[0:ROWS, cols(2, g)] = dvalue.astype(BF)
        both[0:ROWS, cols(1, g)] = dot_t(dkey, perm_ref[...]).astype(BF)
        d_copy(2, g).start()
        d_copy(1, g).start()

    grad_x(0)
    weight_piece(2, GROUPS - 1)
    weight_piece(1, GROUPS - 1)

    grad_x(1)
    first_a = [remote(in_x.at[i], in_x.at[i], send_x.at[i], recv_x.at[i], at(p, y, z, core)) for i, p in enumerate(x_peers)]
    first_b = [remote(in_y.at[i], in_y.at[i], send_y.at[i], recv_y.at[i], at(x, p, z, core)) for i, p in enumerate(y_peers)]
    for copy in first_a:
        copy.wait_recv()
    for j in range(6):
        total = g_buf[6 * x + j, 0:4].astype(F32)
        for i in range(3):
            total += in_x[i, j].astype(F32)
        sum_a[j] = total.astype(BF)
    second_a = [remote(sum_a.at[pl.ds(lax.rem(p, 2) * 3, 3), :, p // 2], in_a.at[i], send_a.at[i], recv_a.at[i],
                       at(x, p, z, core)) for i, p in enumerate(y_peers)]
    for copy in second_a:
        copy.start()
    for copy in first_b:
        copy.wait_recv()
    for px in range(4):
        for j in range(3):
            total = g_buf[px * 6 + y_lo * 3 + j, 4:8, y_hi].astype(F32)
            for i in range(3):
                total += in_y[i, px * 3 + j].astype(F32)
            sum_b[px * 3 + j] = total.astype(BF)
    second_b = [remote(sum_b.at[pl.ds(p * 3, 3)], in_b.at[i], send_b.at[i], recv_b.at[i], at(p, y, z, core))
                for i, p in enumerate(x_peers)]
    for copy in second_b:
        copy.start()
    grad_x(2)
    for copy in second_a:
        copy.wait_recv()
    def halves(rows, blocks):
        middle = blocks[1].astype(BF).astype(F32)
        for c in range(2):
            part = middle[:, :, c * 64:(c + 1) * 64]
            sum_p[rows, c, 0:32] = blocks[2 * c].astype(BF)
            sum_p[rows, c, 32:48] = jnp.concatenate([part[:, :16], part[:, 16:]], axis=2).astype(BF)

    third = [(z, remote(sum_p.at[z, 1 - core], in_z.at[0, core], send_z.at[0, 1 - core], recv_z.at[0, core], partner))]
    for i, p in enumerate(z_peers):
        for c in range(2):
            third.append((p, remote(sum_p.at[p, c], in_z.at[i + 1, core], send_z.at[i + 1, c], recv_z.at[i + 1, core],
                                    at(x, y, p, c))))

    def send_third(upper):
        for p, copy in third:
            @pl.when(p // 4 == upper)
            def _():
                copy.start()

    blocks = []
    for j in range(3):
        total = sum_a[y_lo * 3 + j, :, y_hi].astype(F32)
        for i in range(3):
            total += in_a[i, j].astype(F32)
        blocks.append(total)
    halves(slice(0, 4), blocks)
    send_third(0)
    for copy in second_b:
        copy.wait_recv()
    blocks = []
    for j in range(3):
        total = sum_b[x * 3 + j].astype(F32)
        for i in range(3):
            total += in_b[i, j].astype(F32)
        blocks.append(total)
    halves(slice(4, 8), blocks)
    send_third(1)
    grad_x(3)
    for copy in first_a + first_b + second_a + second_b + x_pair + x_cross + x_pass + u_pair + u_cross + [u_partner, u_pass]:
        copy.wait_send()

    @pl.loop(0, GROUPS)
    def _(g):
        for part in range(3):
            d_copy(part, g).wait_send()
        s_copy(g, 1, partner).wait_send()
        s_copy(g, 2, pair).wait_send()
        s_copy(g, 3, diagonal).wait_send()
        s_copy(g, 4, partner).wait_send()
        out_copy(g).wait()

    for j in range(4):
        gx_copy(j).wait()
    for _, copy in third:
        copy.wait_send()

    def arrived(i, c):
        remote(in_z.at[i, c], in_z.at[i, c], send_z.at[i, c], recv_z.at[i, c], partner).wait_recv()

    for own in (False, True):
        c = core if own else 1 - core
        total = None
        for i in range(8):
            if own and i == 0:
                one = sum_p[z, core]
            else:
                arrived(i, c)
                one = in_z[i, c]
            total = one.astype(F32) if total is None else total + one.astype(F32)
        total = total * (65536.0 ** -0.5)
        whole = total[:32]
        middle = jnp.concatenate([total[32:, :64], total[32:, 64:]], axis=0)
        gw_ref[pl.ds(pl.multiple_of(c * 32, 32), 32), :] = jnp.where(
            core == 0, jnp.concatenate([whole, middle], axis=1), jnp.concatenate([middle, whole], axis=1))


def run_step(listed, x, w, up, spots, freq):
    vmem = pl.BlockSpec(memory_space=pltpu.VMEM)
    hbm = pl.BlockSpec(memory_space=pl.ANY)
    dma = pltpu.SemaphoreType.DMA
    block = jax.ShapeDtypeStruct((ROWS, 1024), BF)
    buffers = [
        ((ROWS, 1024), BF), ((ROWS, 1024), BF),
        ((256, 256), BF), ((SLOTS, ROWS, 1024), BF), ((SLOTS, 1, ROWS), jnp.int32), ((1024, 3072), BF), ((1024, 2048), BF),
        ((SLOTS * ROWS, 1024), BF), ((SLOTS * ROWS, 1024), BF), ((SLOTS * ROWS, 1024), BF), ((SLOTS * ROWS, 1024), BF),
        ((SLOTS, ROWS, 128), F32), ((SLOTS, ROWS, 128), F32), ((SLOTS, GROUPS, 8, ROWS), F32),
        ((2 * ROWS, 3072), BF), ((512, 512), BF),
        ((24, 8, 2, 32, 128), BF), ((3, 6, 4, 2, 32, 128), BF), ((3, 12, 4, 32, 128), BF), ((6, 4, 2, 32, 128), BF),
        ((12, 4, 32, 128), BF), ((3, 3, 4, 32, 128), BF), ((3, 3, 4, 32, 128), BF), ((8, 2, 48, 128), BF),
        ((8, 2, 48, 128), BF),
    ]
    x_moves, u_moves = (2 + 3 * PIECES,), (2 + 2 * PIECES,)
    semaphores = [dma((11,)), dma(x_moves), dma(x_moves), dma((5,)), dma((5,)), dma(u_moves), dma(u_moves)]
    semaphores += [dma((5, GROUPS))] * 2 + [dma((3, GROUPS))] * 2 + [dma((3,))] * 8 + [dma((8, 2))] * 2
    return pl.pallas_call(
        step_kernel,
        in_specs=[pl.BlockSpec(memory_space=pltpu.SMEM), hbm, hbm, hbm, vmem, vmem],
        out_specs=[hbm, hbm, vmem],
        out_shape=[block, block, jax.ShapeDtypeStruct((64, 192), F32)],
        scratch_shapes=[pltpu.VMEM(shape, kind) for shape, kind in buffers] + semaphores,
        compiler_params=pltpu.CompilerParams(collective_id=0, has_side_effects=True, vmem_limit_bytes=63 * 2**20),
        name="whole_step",
    )(listed, x, w, up, spots, freq)


def hand_out_kernel(a_hbm, b_hbm, c_hbm, a_out, b_out, c_out, a_buf, b_buf, c_buf, sems):
    moves = []
    for source, buffer, target, parts in ((a_hbm, a_buf, a_out, 4), (b_hbm, b_buf, b_out, 4), (c_hbm, c_buf, c_out, 1)):
        rows = buffer.shape[0] // parts
        for i in range(parts):
            part = pl.ds(i * rows, rows)
            sem = sems.at[len(moves)]
            moves.append((pltpu.make_async_copy(source.at[part], buffer.at[part], sem),
                          pltpu.make_async_copy(buffer.at[part], target.at[part], sem)))
    for bring, _ in moves:
        bring.start()
    for bring, give in moves:
        bring.wait()
        give.start()
    for _, give in moves:
        give.wait()


def hand_out(a, b, c):
    hbm = pl.BlockSpec(memory_space=pl.ANY)
    arrays = (a, b, c)
    return pl.pallas_call(
        hand_out_kernel,
        in_specs=[hbm] * 3,
        out_specs=[hbm] * 3,
        out_shape=[jax.ShapeDtypeStruct(one.shape, one.dtype) for one in arrays],
        scratch_shapes=[pltpu.VMEM(one.shape, one.dtype) for one in arrays] + [pltpu.SemaphoreType.DMA((9,))],
        name="hand_out",
    )(*arrays)


def per_device(features, w_qkv, grad_out, positions, block_list):
    frequency = np.float32(INTERP) * np.float32(BASE) ** (np.float32(-2.0) * np.arange(32, dtype=np.float32) / np.float32(64))
    freq = jnp.asarray(np.broadcast_to(np.tile(frequency, 4), (8, 128)))
    out, grad_x, grad_w = hand_out(*run_step(block_list, features[0], w_qkv, grad_out[0], positions, freq))
    return (out[None], grad_x[None], grad_w)


def solution(mesh):
    return jax.shard_map(
        per_device,
        mesh=mesh,
        in_specs=(
            P("dates", "lon", None),
            P(),
            P("dates", "lon", None),
            P("dates", "lon"),
            P("dates", None),
        ),
        out_specs=(P("dates", "lon", None), P("dates", "lon", None), P("dates", "lon")),
        check_vma=False,
    )
```

```python
import jax
import jax.numpy as jnp
import numpy as np
from jax import lax
from jax.experimental import pallas as pl
from jax.experimental.pallas import tpu as pltpu
from jax.sharding import PartitionSpec as P

INTERP = 0.25
BASE = 10000.0
FAR = 1e30
LOG2E = 1.4426950408889634
FREQUENCY = [float(np.float32(INTERP) * np.float32(BASE) ** np.float32(-2.0 * j / 64)) for j in range(32)]
BF = jnp.bfloat16
F32 = jnp.float32
MESH = pl.DeviceIdType.MESH
ROWS = 256
GROUPS = 4
SLOTS = 5
PIECES = 4


def dot(a, b):
    return lax.dot_general(a, b, (((1,), (0,)), ((), ())), preferred_element_type=F32)


def dot_t(a, b):
    return lax.dot_general(a, b, (((1,), (1,)), ((), ())), preferred_element_type=F32)


def lanes(shape):
    return lax.broadcasted_iota(jnp.int32, shape, len(shape) - 1)


def perm_matrix():
    source = lax.broadcasted_iota(jnp.int32, (256, 256), 0)
    column = lax.broadcasted_iota(jnp.int32, (256, 256), 1)
    wanted = (column // 32 % 4) * 64 + (column // 128) * 32 + column % 32
    return jnp.where(source == wanted, 1.0, 0.0).astype(BF)


def turn(value, cosine, sine):
    a, c = value[:, :128], value[:, 128:]
    return jnp.concatenate([a * cosine - c * sine, a * sine + c * cosine], axis=1)


def turn_back(value, cosine, sine):
    a, c = value[:, :128], value[:, 128:]
    return jnp.concatenate([a * cosine + c * sine, c * cosine - a * sine], axis=1)


def step_kernel(list_hbm, x_hbm, w_hbm, up_hbm, spots_hbm,
                out_hbm, gx_hbm, gw_hbm,
                list_ref, out_ref, gx_ref, gw_ref,
                perm_ref, xs, spots, wbuf, wpair, upbuf, qbuf, kbuf, vbuf, cos5, sin5, stats, both, xt,
                g_buf, in_x, in_y, sum_a, sum_b, in_a, in_b, sum_p, in_z,
                local, x_send, x_recv, p_send, p_recv, u_send, u_recv, s_send, s_recv, d_send, d_recv,
                send_x, recv_x, send_y, recv_y, send_a, recv_a, send_b, recv_b, send_z, recv_z):
    lon, dates = lax.axis_index("lon"), lax.axis_index("dates")
    x, y_lo, core = lon // 4, lax.rem(lon // 2, 2), lax.rem(lon, 2)
    z, y_hi = dates // 2, lax.rem(dates, 2)
    y = y_hi * 2 + y_lo
    step = 1 - 2 * y_lo

    def at(px, py, pz, pc):
        return {"lon": lax.rem(px + 4, 4) * 4 + lax.rem(py, 2) * 2 + pc, "dates": pz * 2 + py // 2}

    other_y = y_hi * 2 + 1 - y_lo
    partner = at(x, y, z, 1 - core)
    pair = at(x, other_y, z, core)
    onward = at(x + step, y, z, core)
    diagonal = at(x - step, other_y, z, core)
    passing = 2 + lax.rem(core + y_lo, 2)
    x_peers = [lax.rem(x + i, 4) for i in (1, 2, 3)]
    y_peers = [lax.rem(y + i, 4) for i in (1, 2, 3)]
    z_peers = [lax.rem(z + i, 8) for i in range(1, 8)]

    bring = [pltpu.make_async_copy(x_hbm, xs.at[0], local.at[0]),
             pltpu.make_async_copy(w_hbm, wbuf, local.at[1]),
             pltpu.make_async_copy(up_hbm, upbuf.at[pl.ds(0, ROWS)], local.at[2]),
             pltpu.make_async_copy(spots_hbm, spots.at[0], local.at[11]),
             pltpu.make_async_copy(list_hbm, list_ref, local.at[12])]
    for copy in bring:
        copy.start()
    barrier = pltpu.get_barrier_semaphore()
    peers = [partner, diagonal] + [at(p, y, z, core) for p in x_peers] + [at(x, p, z, core) for p in y_peers]
    peers += [at(x, y, p, c) for p in z_peers for c in range(2)]
    for peer in peers:
        pl.semaphore_signal(barrier, inc=1, device_id=peer, device_id_type=MESH)
    pl.semaphore_wait(barrier, len(peers))

    offsets = (0, 1 - 2 * core, 2 * step, -2 * step, 2 * core - 1)

    def bias(offset):
        found = list_ref[0, 0] == offset
        for i in range(1, 5):
            found = jnp.logical_or(found, list_ref[0, i] == offset)
        return jnp.where(found, 0.0, FAR)

    def remote(source, target, send_sem, recv_sem, peer):
        return pltpu.make_async_remote_copy(src_ref=source, dst_ref=target, send_sem=send_sem, recv_sem=recv_sem,
                                            device_id=peer, device_id_type=MESH)

    routes = ((1, partner), (2, pair), (3, diagonal))
    p_copies = {slot: remote(spots_hbm, spots.at[slot], p_send.at[slot], p_recv.at[slot], peer) for slot, peer in routes}
    p_copies[4] = remote(spots.at[passing], spots.at[4], p_send.at[4], p_recv.at[4], partner)

    def piece(j):
        return pl.ds(j * (ROWS // PIECES), ROWS // PIECES)

    x_partner = remote(x_hbm, xs.at[1], x_send.at[0], x_recv.at[0], partner)
    x_pair = [remote(x_hbm.at[piece(j)], xs.at[2, piece(j)], x_send.at[2 + j], x_recv.at[2 + j], pair)
              for j in range(PIECES)]
    x_cross = [remote(xs.at[2, piece(j)], xs.at[3, piece(j)], x_send.at[2 + PIECES + j], x_recv.at[2 + PIECES + j], onward)
               for j in range(PIECES)]
    x_pass = [remote(xs.at[passing, piece(j)], xs.at[4, piece(j)], x_send.at[2 + 2 * PIECES + j],
                     x_recv.at[2 + 2 * PIECES + j], partner) for j in range(PIECES)]

    def block(slot):
        return pl.ds(pl.multiple_of(slot * ROWS, ROWS), ROWS)

    def block_piece(slot, j):
        return pl.ds(slot * ROWS + j * (ROWS // PIECES), ROWS // PIECES)

    u_partner = remote(up_hbm, upbuf.at[block(1)], u_send.at[0], u_recv.at[0], partner)
    u_pass = remote(upbuf.at[block(passing)], upbuf.at[block(4)], u_send.at[1], u_recv.at[1], partner)
    u_pair = [remote(up_hbm.at[piece(j)], upbuf.at[block_piece(2, j)], u_send.at[2 + j], u_recv.at[2 + j], pair)
              for j in range(PIECES)]
    u_cross = [remote(upbuf.at[block_piece(2, j)], upbuf.at[block_piece(3, j)], u_send.at[2 + PIECES + j],
                      u_recv.at[2 + PIECES + j], onward) for j in range(PIECES)]
    for slot in (1, 2, 3):
        p_copies[slot].start()
    for copy in x_pair:
        copy.start()
    x_partner.start()
    for copy in u_pair:
        copy.start()
    u_partner.start()

    perm_ref[...] = perm_matrix()
    bring[0].wait()
    bring[1].wait()

    def cols(part, g):
        return pl.ds(pl.multiple_of(part * 1024 + g * 256, 256), 256)

    @pl.loop(0, 2 * GROUPS)
    def _(g):
        wpair[:, cols(0, g)] = dot(wbuf[:, cols(0, g)], perm_ref[...]).astype(BF)

    pair_index = lax.rem(lanes((1, 128)), 32)
    frequency = jnp.zeros((1, 128), F32)
    for j, one in enumerate(FREQUENCY):
        frequency = jnp.where(pair_index == j, one, frequency)

    def tables(slot, row):
        spread = jnp.broadcast_to(row.astype(F32), (128, ROWS)).T
        angle = spread * frequency
        cos5[slot] = jnp.cos(angle)
        sin5[slot] = jnp.sin(angle)

    def project(slot):
        into = block(slot)

        @pl.loop(0, GROUPS)
        def _(g):
            tokens = xs[slot]
            cosine, sine = cos5[slot], sin5[slot]
            query = turn(dot(tokens, wpair[:, cols(0, g)]), cosine, sine).astype(BF).astype(F32) * 0.125
            qbuf[into, cols(0, g)] = query.astype(BF)
            kbuf[into, cols(0, g)] = turn(dot(tokens, wpair[:, cols(1, g)]), cosine, sine).astype(BF)
            vbuf[into, cols(0, g)] = dot(tokens, wbuf[:, cols(2, g)]).astype(BF)

    def hand_on(j):
        x_pair[j].wait_recv()
        x_cross[j].start()

    def stripes(slot):
        row = lax.broadcasted_iota(jnp.int32, (128, 256), 0)
        chosen = lanes((128, 256)) == row // 32 * 64 + core * 32 + row % 32
        select = jnp.where(chosen, 1.0, 0.0).astype(BF)
        for g in range(GROUPS):
            xt[g * 128:(g + 1) * 128, slot * ROWS:(slot + 1) * ROWS] = dot_t(select, xs[slot, :, g * 256:(g + 1) * 256]).astype(BF)

    def hand_on_up(j):
        u_pair[j].wait_recv()
        u_cross[j].start()

    bring[3].wait()
    bring[4].wait()
    bias_to = [bias(offset) for offset in offsets]
    bias_from = [bias(-offset) for offset in offsets]
    tables(0, spots[0])
    hand_on(0)
    project(0)
    hand_on(1)
    p_copies[1].wait()
    tables(1, spots[1])
    x_partner.wait()
    project(1)
    hand_on(2)
    p_copies[2].wait()
    p_copies[3].wait()
    p_copies[4].start()
    tables(2, spots[2])
    tables(3, spots[3])
    hand_on(3)
    project(2)
    p_copies[4].wait()
    tables(4, spots[4])
    stripes(0)
    stripes(1)
    for cross, passed in zip(x_cross, x_pass):
        cross.wait_recv()
        passed.start()
    project(3)
    hand_on_up(0)
    bring[2].wait()
    for copy in x_pass:
        copy.wait_recv()
    project(4)
    hand_on_up(1)
    lane = lanes((ROWS, 256))
    lane_pair = lane // 32 % 4
    lane_flat = lane // 64
    stat_lane = lanes((ROWS, 128))
    zero = jnp.zeros((), BF)

    def s_copy(g, slot, peer):
        return remote(stats.at[passing if slot == 4 else 0, g], stats.at[slot, g],
                      s_send.at[slot, g], s_recv.at[slot, g], peer)

    def d_copy(part, g):
        return remote(both.at[pl.ds(0, ROWS), cols(part, g)], both.at[pl.ds(ROWS, ROWS), cols(part, g)],
                      d_send.at[part, g], d_recv.at[part, g], partner)

    def send_first(s):
        px, lo = s // 6, lax.rem(s // 3, 2)

        @pl.when(px != x)
        def _():
            slot = lax.rem(px - x + 3, 4)
            remote(g_buf.at[s, pl.ds(0, 4)], in_x.at[slot, s - 6 * px], send_x.at[slot], recv_x.at[slot],
                   at(px, y, z, core)).start()

        for hi in range(2):
            py = hi * 2 + lo

            @pl.when(py != y)
            def _():
                slot = lax.rem(py - y + 3, 4)
                remote(g_buf.at[s, pl.ds(4, 4), hi], in_y.at[slot, px * 3 + lax.rem(s, 3)], send_y.at[slot],
                       recv_y.at[slot], at(x, py, z, core)).start()

    def weight_piece(part, g):
        d_copy(part, g).wait_recv()
        value = dot(xt[...], both[:, cols(part, g)]).astype(BF)
        first = part * 8 + g * 2
        g_buf[first] = value[:, :128].reshape(8, 2, 32, 128)
        g_buf[first + 1] = value[:, 128:].reshape(8, 2, 32, 128)
        send_first(first)
        send_first(first + 1)

    def pass_stats(g):
        s_copy(g, 2, pair).wait_recv()
        s_copy(g, 3, diagonal).wait_recv()
        s_copy(g, 4, partner).start()

    def out_copy(g):
        return pltpu.make_async_copy(out_ref.at[:, cols(0, g)], out_hbm.at[:, cols(0, g)], local.at[3 + g])

    @pl.loop(0, GROUPS)
    def _(g):
        mid = cols(0, g)
        query = qbuf[block(0), mid]
        up_g = upbuf[block(0), mid]
        out = jnp.zeros((ROWS, 256), F32)
        dquery = jnp.zeros((ROWS, 256), F32)
        now = jnp.zeros((ROWS, 128), F32)
        for head in range(4):
            own_pair = lane_pair == head
            own_flat = lane_flat == head
            scores = dot_t(jnp.where(own_pair, query, zero), kbuf[:, mid])
            row_max = None
            for slot in range(SLOTS):
                left = slot * ROWS
                one = jnp.maximum(scores[:, left:left + 128], scores[:, left + 128:left + 256]) - bias_to[slot]
                row_max = one if row_max is None else jnp.maximum(row_max, one)
            row_max = jnp.max(row_max, axis=1, keepdims=True)
            parts = []
            total = None
            for slot in range(SLOTS):
                one = jnp.exp2((scores[:, slot * ROWS:(slot + 1) * ROWS] - (row_max + bias_to[slot])) * LOG2E)
                part_sum = one[:, :128] + one[:, 128:]
                total = part_sum if total is None else total + part_sum
                parts.append(one)
            total = jnp.sum(total, axis=1, keepdims=True)
            weights = jnp.concatenate(parts, axis=1)
            inverse = 1.0 / total
            attended = dot(weights.astype(BF), vbuf[:, mid]) * inverse
            attended = attended.astype(BF).astype(F32)
            out = jnp.where(own_flat, attended, out)
            up_own = jnp.where(own_flat, up_g, zero)
            delta = jnp.sum(up_own.astype(F32) * attended, axis=1, keepdims=True)
            dprobs = dot_t(up_own, vbuf[:, mid])
            dscores = (weights * (dprobs - delta)).astype(BF)
            dquery = jnp.where(own_pair, dot(dscores, kbuf[:, mid]) * (inverse * 0.125), dquery)
            now = jnp.where(stat_lane == head, row_max * LOG2E + jnp.log2(total), now)
            now = jnp.where(stat_lane == head + 4, delta, now)
        stats[0, g] = now.T[:8]
        dquery = turn_back(dquery, cos5[0], sin5[0]).astype(BF)
        both[0:ROWS, mid] = dot_t(dquery, perm_ref[...]).astype(BF)
        out_ref[:, mid] = out.astype(BF)
        for slot, peer in routes:
            s_copy(g, slot, peer).start()
        d_copy(0, g).start()
        out_copy(g).start()

        @pl.when(g == 0)
        def _():
            hand_on_up(2)
            hand_on_up(3)

        @pl.when(g == 2)
        def _():
            for copy in u_cross:
                copy.wait_recv()
            u_pass.start()

        @pl.when(g > 0)
        def _():
            pass_stats(g - 1)
            weight_piece(0, g - 1)

    def gx_copy(j):
        return pltpu.make_async_copy(gx_ref.at[:, pl.ds(j * 256, 256)], gx_hbm.at[:, pl.ds(j * 256, 256)], local.at[7 + j])

    def grad_x(j):
        rows = slice(j * 256, (j + 1) * 256)
        gx_ref[:, rows] = dot_t(both[0:ROWS], wbuf[rows]).astype(BF)
        gx_copy(j).start()

    def nth(turn_no):
        return lax.rem(turn_no + lax.div(turn_no + 2, 3) + lax.div(turn_no, 3), GROUPS)

    @pl.loop(0, GROUPS)
    def _(turn_no):
        g = nth(turn_no)
        earlier = nth(lax.rem(turn_no + 3, GROUPS))
        mid = cols(0, g)
        s_copy(g, 1, partner).wait_recv()
        s_copy(g, 4, partner).wait_recv()

        @pl.when(turn_no == 0)
        def _():
            u_partner.wait_recv()
            u_pass.wait_recv()

        key, value = kbuf[block(0), mid], vbuf[block(0), mid]
        dkey = jnp.zeros((ROWS, 256), F32)
        dvalue = jnp.zeros((ROWS, 256), F32)
        for head in range(4):
            own_pair = lane_pair == head
            own_flat = lane_flat == head
            lse = jnp.concatenate([stats[slot, g, head:head + 1] + bias_from[slot] for slot in range(SLOTS)], axis=1)
            delta = jnp.concatenate([stats[slot, g, head + 4:head + 5] for slot in range(SLOTS)], axis=1)
            scores = dot_t(jnp.where(own_pair, key, zero), qbuf[:, mid]) * LOG2E
            probs = jnp.exp2(scores - lse)
            dprobs = dot_t(jnp.where(own_flat, value, zero), upbuf[:, mid])
            dscores = (probs * (dprobs - delta)).astype(BF)
            dvalue = jnp.where(own_flat, dot(probs.astype(BF), upbuf[:, mid]), dvalue)
            dkey = jnp.where(own_pair, dot(dscores, qbuf[:, mid]), dkey)
            if head == 2:
                @pl.when(turn_no == 0)
                def _():
                    pass_stats(GROUPS - 1)
                    weight_piece(0, GROUPS - 1)

                @pl.when(turn_no > 0)
                def _():
                    weight_piece(2, earlier)
                    weight_piece(1, earlier)
        dkey = turn_back(dkey, cos5[0], sin5[0]).astype(BF)
        both[0:ROWS, cols(2, g)] = dvalue.astype(BF)
        both[0:ROWS, cols(1, g)] = dot_t(dkey, perm_ref[...]).astype(BF)
        d_copy(2, g).start()
        d_copy(1, g).start()

    grad_x(0)
    weight_piece(2, 1)
    weight_piece(1, 1)

    grad_x(1)
    first_a = [remote(in_x.at[i], in_x.at[i], send_x.at[i], recv_x.at[i], at(p, y, z, core)) for i, p in enumerate(x_peers)]
    first_b = [remote(in_y.at[i], in_y.at[i], send_y.at[i], recv_y.at[i], at(x, p, z, core)) for i, p in enumerate(y_peers)]
    for copy in first_a:
        copy.wait_recv()
    for j in range(6):
        total = g_buf[6 * x + j, 0:4].astype(F32)
        for i in range(3):
            total += in_x[i, j].astype(F32)
        sum_a[j] = total.astype(BF)
    second_a = [remote(sum_a.at[pl.ds(lax.rem(p, 2) * 3, 3), :, p // 2], in_a.at[i], send_a.at[i], recv_a.at[i],
                       at(x, p, z, core)) for i, p in enumerate(y_peers)]
    for copy in second_a:
        copy.start()
    for copy in first_b:
        copy.wait_recv()
    for px in range(4):
        for j in range(3):
            total = g_buf[px * 6 + y_lo * 3 + j, 4:8, y_hi].astype(F32)
            for i in range(3):
                total += in_y[i, px * 3 + j].astype(F32)
            sum_b[px * 3 + j] = total.astype(BF)
    second_b = [remote(sum_b.at[pl.ds(p * 3, 3)], in_b.at[i], send_b.at[i], recv_b.at[i], at(p, y, z, core))
                for i, p in enumerate(x_peers)]
    for copy in second_b:
        copy.start()
    grad_x(2)
    for copy in second_a:
        copy.wait_recv()
    def halves(rows, blocks):
        middle = blocks[1].astype(BF).astype(F32)
        for c in range(2):
            part = middle[:, :, c * 64:(c + 1) * 64]
            sum_p[rows, c, 0:32] = blocks[2 * c].astype(BF)
            sum_p[rows, c, 32:48] = jnp.concatenate([part[:, :16], part[:, 16:]], axis=2).astype(BF)

    third = [(z, remote(sum_p.at[z, 1 - core], in_z.at[0, core], send_z.at[0, 1 - core], recv_z.at[0, core], partner))]
    for i, p in enumerate(z_peers):
        for c in range(2):
            third.append((p, remote(sum_p.at[p, c], in_z.at[i + 1, core], send_z.at[i + 1, c], recv_z.at[i + 1, core],
                                    at(x, y, p, c))))

    def send_third(upper):
        for p, copy in third:
            @pl.when(p // 4 == upper)
            def _():
                copy.start()

    blocks = []
    for j in range(3):
        total = sum_a[y_lo * 3 + j, :, y_hi].astype(F32)
        for i in range(3):
            total += in_a[i, j].astype(F32)
        blocks.append(total)
    halves(slice(0, 4), blocks)
    send_third(0)
    for copy in second_b:
        copy.wait_recv()
    blocks = []
    for j in range(3):
        total = sum_b[x * 3 + j].astype(F32)
        for i in range(3):
            total += in_b[i, j].astype(F32)
        blocks.append(total)
    halves(slice(4, 8), blocks)
    send_third(1)
    grad_x(3)
    for copy in first_a + first_b + second_a + second_b + x_pair + x_cross + x_pass + u_pair + u_cross + [u_partner, u_pass]:
        copy.wait_send()

    @pl.loop(0, GROUPS)
    def _(g):
        for part in range(3):
            d_copy(part, g).wait_send()
        s_copy(g, 1, partner).wait_send()
        s_copy(g, 2, pair).wait_send()
        s_copy(g, 3, diagonal).wait_send()
        s_copy(g, 4, partner).wait_send()
        out_copy(g).wait()

    for j in range(4):
        gx_copy(j).wait()
    for _, copy in third:
        copy.wait_send()

    def arrived(i, c):
        remote(in_z.at[i, c], in_z.at[i, c], send_z.at[i, c], recv_z.at[i, c], partner).wait_recv()

    give = []
    for own in (False, True):
        c = core if own else 1 - core
        total = None
        for i in range(8):
            if own and i == 0:
                one = sum_p[z, core]
            else:
                arrived(i, c)
                one = in_z[i, c]
            total = one.astype(F32) if total is None else total + one.astype(F32)
        total = total * (65536.0 ** -0.5)
        whole = total[:32]
        middle = jnp.concatenate([total[32:, :64], total[32:, 64:]], axis=0)
        gw_ref[pl.ds(pl.multiple_of(c * 32, 32), 32), :] = jnp.where(
            core == 0, jnp.concatenate([whole, middle], axis=1), jnp.concatenate([middle, whole], axis=1))
        done = pl.ds(pl.multiple_of(c * 32, 32), 32)
        give.append(pltpu.make_async_copy(gw_ref.at[done], gw_hbm.at[done], local.at[13 + own]))
        give[-1].start()
    for copy in give:
        copy.wait()


def run_step(listed, x, w, up, spots):
    hbm = pl.BlockSpec(memory_space=pl.ANY)
    dma = pltpu.SemaphoreType.DMA
    block = jax.ShapeDtypeStruct((ROWS, 1024), BF)
    buffers = [
        ((ROWS, 1024), BF), ((ROWS, 1024), BF), ((64, 192), F32),
        ((256, 256), BF), ((SLOTS, ROWS, 1024), BF), ((SLOTS, 1, ROWS), jnp.int32), ((1024, 3072), BF), ((1024, 2048), BF),
        ((SLOTS * ROWS, 1024), BF), ((SLOTS * ROWS, 1024), BF), ((SLOTS * ROWS, 1024), BF), ((SLOTS * ROWS, 1024), BF),
        ((SLOTS, ROWS, 128), F32), ((SLOTS, ROWS, 128), F32), ((SLOTS, GROUPS, 8, ROWS), F32),
        ((2 * ROWS, 3072), BF), ((512, 512), BF),
        ((24, 8, 2, 32, 128), BF), ((3, 6, 4, 2, 32, 128), BF), ((3, 12, 4, 32, 128), BF), ((6, 4, 2, 32, 128), BF),
        ((12, 4, 32, 128), BF), ((3, 3, 4, 32, 128), BF), ((3, 3, 4, 32, 128), BF), ((8, 2, 48, 128), BF),
        ((8, 2, 48, 128), BF),
    ]
    x_moves, u_moves = (2 + 3 * PIECES,), (2 + 2 * PIECES,)
    semaphores = [dma((15,)), dma(x_moves), dma(x_moves), dma((5,)), dma((5,)), dma(u_moves), dma(u_moves)]
    semaphores += [dma((5, GROUPS))] * 2 + [dma((3, GROUPS))] * 2 + [dma((3,))] * 8 + [dma((8, 2))] * 2
    return pl.pallas_call(
        step_kernel,
        in_specs=[hbm] * 5,
        out_specs=[hbm] * 3,
        out_shape=[block, block, jax.ShapeDtypeStruct((64, 192), F32)],
        scratch_shapes=[pltpu.SMEM((1, 5), jnp.int32)] + [pltpu.VMEM(shape, kind) for shape, kind in buffers] + semaphores,
        compiler_params=pltpu.CompilerParams(collective_id=0, has_side_effects=True, vmem_limit_bytes=63 * 2**20),
        name="whole_step",
    )(listed, x, w, up, spots)


def hand_out_kernel(a_hbm, b_hbm, c_hbm, a_out, b_out, c_out, a_buf, b_buf, c_buf, sems):
    moves = []
    for source, buffer, target, parts in ((a_hbm, a_buf, a_out, 4), (b_hbm, b_buf, b_out, 4), (c_hbm, c_buf, c_out, 1)):
        rows = buffer.shape[0] // parts
        for i in range(parts):
            part = pl.ds(i * rows, rows)
            sem = sems.at[len(moves)]
            moves.append((pltpu.make_async_copy(source.at[part], buffer.at[part], sem),
                          pltpu.make_async_copy(buffer.at[part], target.at[part], sem)))
    for bring, _ in moves:
        bring.start()
    for bring, give in moves:
        bring.wait()
        give.start()
    for _, give in moves:
        give.wait()


def hand_out(a, b, c):
    hbm = pl.BlockSpec(memory_space=pl.ANY)
    arrays = (a, b, c)
    return pl.pallas_call(
        hand_out_kernel,
        in_specs=[hbm] * 3,
        out_specs=[hbm] * 3,
        out_shape=[jax.ShapeDtypeStruct(one.shape, one.dtype) for one in arrays],
        scratch_shapes=[pltpu.VMEM(one.shape, one.dtype) for one in arrays] + [pltpu.SemaphoreType.DMA((9,))],
        name="hand_out",
    )(*arrays)


def per_device(features, w_qkv, grad_out, positions, block_list):
    out, grad_x, grad_w = hand_out(*run_step(block_list, features[0], w_qkv, grad_out[0], positions))
    return (out[None], grad_x[None], grad_w)


def solution(mesh):
    return jax.shard_map(
        per_device,
        mesh=mesh,
        in_specs=(
            P("dates", "lon", None),
            P(),
            P("dates", "lon", None),
            P("dates", "lon"),
            P("dates", None),
        ),
        out_specs=(P("dates", "lon", None), P("dates", "lon", None), P("dates", "lon")),
        check_vma=False,
    )
```

```python
import jax
import jax.numpy as jnp
import numpy as np
from jax import lax
from jax.experimental import pallas as pl
from jax.experimental.pallas import tpu as pltpu
from jax.sharding import PartitionSpec as P

INTERP = 0.25
BASE = 10000.0
FAR = 1e30
LOG2E = 1.4426950408889634
FREQUENCY = [float(np.float32(INTERP) * np.float32(BASE) ** np.float32(-2.0 * j / 64)) for j in range(32)]
BF = jnp.bfloat16
F32 = jnp.float32
MESH = pl.DeviceIdType.MESH
ROWS = 256
GROUPS = 4
SLOTS = 5
PIECES = 4


def dot(a, b):
    return lax.dot_general(a, b, (((1,), (0,)), ((), ())), preferred_element_type=F32)


def dot_t(a, b):
    return lax.dot_general(a, b, (((1,), (1,)), ((), ())), preferred_element_type=F32)


def lanes(shape):
    return lax.broadcasted_iota(jnp.int32, shape, len(shape) - 1)


def perm_matrix():
    source = lax.broadcasted_iota(jnp.int32, (256, 256), 0)
    column = lax.broadcasted_iota(jnp.int32, (256, 256), 1)
    wanted = (column // 32 % 4) * 64 + (column // 128) * 32 + column % 32
    return jnp.where(source == wanted, 1.0, 0.0).astype(BF)


def turn(value, cosine, sine):
    a, c = value[:, :128], value[:, 128:]
    return jnp.concatenate([a * cosine - c * sine, a * sine + c * cosine], axis=1)


def turn_back(value, cosine, sine):
    a, c = value[:, :128], value[:, 128:]
    return jnp.concatenate([a * cosine + c * sine, c * cosine - a * sine], axis=1)


def step_kernel(list_hbm, x_hbm, w_hbm, up_hbm, spots_hbm,
                out_hbm, gx_hbm, gw_hbm,
                list_ref, out_ref, gx_ref, gw_ref,
                perm_ref, xs, spots, wbuf, wpair, upbuf, qbuf, kbuf, vbuf, cos5, sin5, stats, both, xt,
                g_buf, in_x, in_y, sum_a, sum_b, in_a, in_b, sum_p, in_z,
                local, x_send, x_recv, p_send, p_recv, u_send, u_recv, s_send, s_recv, d_send, d_recv,
                send_x, recv_x, send_y, recv_y, send_a, recv_a, send_b, recv_b, send_z, recv_z):
    lon, dates = lax.axis_index("lon"), lax.axis_index("dates")
    x, y_lo, core = lon // 4, lax.rem(lon // 2, 2), lax.rem(lon, 2)
    z, y_hi = dates // 2, lax.rem(dates, 2)
    y = y_hi * 2 + y_lo
    step = 1 - 2 * y_lo

    def at(px, py, pz, pc):
        return {"lon": lax.rem(px + 4, 4) * 4 + lax.rem(py, 2) * 2 + pc, "dates": pz * 2 + py // 2}

    other_y = y_hi * 2 + 1 - y_lo
    partner = at(x, y, z, 1 - core)
    pair = at(x, other_y, z, core)
    onward = at(x + step, y, z, core)
    diagonal = at(x - step, other_y, z, core)
    passing = 2 + lax.rem(core + y_lo, 2)
    x_peers = [lax.rem(x + i, 4) for i in (1, 2, 3)]
    y_peers = [lax.rem(y + i, 4) for i in (1, 2, 3)]
    z_peers = [lax.rem(z + i, 8) for i in range(1, 8)]

    bring = [pltpu.make_async_copy(x_hbm, xs.at[0], local.at[0]),
             pltpu.make_async_copy(w_hbm, wbuf, local.at[1]),
             pltpu.make_async_copy(up_hbm, upbuf.at[pl.ds(0, ROWS)], local.at[2]),
             pltpu.make_async_copy(spots_hbm, spots.at[0], local.at[11]),
             pltpu.make_async_copy(list_hbm, list_ref, local.at[12])]
    for copy in bring:
        copy.start()
    barrier = pltpu.get_barrier_semaphore()
    peers = [partner, diagonal] + [at(p, y, z, core) for p in x_peers] + [at(x, p, z, core) for p in y_peers]
    peers += [at(x, y, p, c) for p in z_peers for c in range(2)]
    for peer in peers:
        pl.semaphore_signal(barrier, inc=1, device_id=peer, device_id_type=MESH)
    pl.semaphore_wait(barrier, len(peers))

    offsets = (0, 1 - 2 * core, 2 * step, -2 * step, 2 * core - 1)

    def bias(offset):
        found = list_ref[0, 0] == offset
        for i in range(1, 5):
            found = jnp.logical_or(found, list_ref[0, i] == offset)
        return jnp.where(found, 0.0, FAR)

    def remote(source, target, send_sem, recv_sem, peer):
        return pltpu.make_async_remote_copy(src_ref=source, dst_ref=target, send_sem=send_sem, recv_sem=recv_sem,
                                            device_id=peer, device_id_type=MESH)

    routes = ((1, partner), (2, pair), (3, diagonal))
    p_copies = {slot: remote(spots_hbm, spots.at[slot], p_send.at[slot], p_recv.at[slot], peer) for slot, peer in routes}
    p_copies[4] = remote(spots.at[passing], spots.at[4], p_send.at[4], p_recv.at[4], partner)

    def piece(j):
        return pl.ds(j * (ROWS // PIECES), ROWS // PIECES)

    x_partner = remote(x_hbm, xs.at[1], x_send.at[0], x_recv.at[0], partner)
    x_pair = [remote(x_hbm.at[piece(j)], xs.at[2, piece(j)], x_send.at[2 + j], x_recv.at[2 + j], pair)
              for j in range(PIECES)]
    x_cross = [remote(xs.at[2, piece(j)], xs.at[3, piece(j)], x_send.at[2 + PIECES + j], x_recv.at[2 + PIECES + j], onward)
               for j in range(PIECES)]
    x_pass = [remote(xs.at[passing, piece(j)], xs.at[4, piece(j)], x_send.at[2 + 2 * PIECES + j],
                     x_recv.at[2 + 2 * PIECES + j], partner) for j in range(PIECES)]

    def block(slot):
        return pl.ds(pl.multiple_of(slot * ROWS, ROWS), ROWS)

    def block_piece(slot, j):
        return pl.ds(slot * ROWS + j * (ROWS // PIECES), ROWS // PIECES)

    u_partner = remote(up_hbm, upbuf.at[block(1)], u_send.at[0], u_recv.at[0], partner)
    u_pass = remote(upbuf.at[block(passing)], upbuf.at[block(4)], u_send.at[1], u_recv.at[1], partner)
    u_pair = [remote(up_hbm.at[piece(j)], upbuf.at[block_piece(2, j)], u_send.at[2 + j], u_recv.at[2 + j], pair)
              for j in range(PIECES)]
    u_cross = [remote(upbuf.at[block_piece(2, j)], upbuf.at[block_piece(3, j)], u_send.at[2 + PIECES + j],
                      u_recv.at[2 + PIECES + j], onward) for j in range(PIECES)]
    for slot in (1, 2, 3):
        p_copies[slot].start()
    for copy in x_pair:
        copy.start()
    x_partner.start()
    for copy in u_pair:
        copy.start()
    u_partner.start()

    perm_ref[...] = perm_matrix()
    bring[0].wait()
    bring[1].wait()

    def cols(part, g):
        return pl.ds(pl.multiple_of(part * 1024 + g * 256, 256), 256)

    @pl.loop(0, 2 * GROUPS)
    def _(g):
        wpair[:, cols(0, g)] = dot(wbuf[:, cols(0, g)], perm_ref[...]).astype(BF)

    pair_index = lax.rem(lanes((1, 128)), 32)
    frequency = jnp.zeros((1, 128), F32)
    for j, one in enumerate(FREQUENCY):
        frequency = jnp.where(pair_index == j, one, frequency)

    def tables(slot, row):
        spread = jnp.broadcast_to(row.astype(F32), (128, ROWS)).T
        angle = spread * frequency
        cos5[slot] = jnp.cos(angle)
        sin5[slot] = jnp.sin(angle)

    def project(slot):
        into = block(slot)

        @pl.loop(0, GROUPS)
        def _(g):
            tokens = xs[slot]
            cosine, sine = cos5[slot], sin5[slot]
            query = turn(dot(tokens, wpair[:, cols(0, g)]), cosine, sine).astype(BF).astype(F32) * 0.125
            qbuf[into, cols(0, g)] = query.astype(BF)
            kbuf[into, cols(0, g)] = turn(dot(tokens, wpair[:, cols(1, g)]), cosine, sine).astype(BF)
            vbuf[into, cols(0, g)] = dot(tokens, wbuf[:, cols(2, g)]).astype(BF)

    def hand_on(j):
        x_pair[j].wait_recv()
        x_cross[j].start()

    def stripes(slot):
        row = lax.broadcasted_iota(jnp.int32, (128, 256), 0)
        chosen = lanes((128, 256)) == row // 32 * 64 + core * 32 + row % 32
        select = jnp.where(chosen, 1.0, 0.0).astype(BF)
        for g in range(GROUPS):
            xt[g * 128:(g + 1) * 128, slot * ROWS:(slot + 1) * ROWS] = dot_t(select, xs[slot, :, g * 256:(g + 1) * 256]).astype(BF)

    def hand_on_up(j):
        u_pair[j].wait_recv()
        u_cross[j].start()

    bring[3].wait()
    bring[4].wait()
    bias_to = [bias(offset) for offset in offsets]
    bias_from = [bias(-offset) for offset in offsets]
    tables(0, spots[0])
    hand_on(0)
    project(0)
    hand_on(1)
    p_copies[1].wait()
    tables(1, spots[1])
    x_partner.wait()
    project(1)
    hand_on(2)
    p_copies[2].wait()
    p_copies[3].wait()
    p_copies[4].start()
    tables(2, spots[2])
    tables(3, spots[3])
    hand_on(3)
    project(2)
    p_copies[4].wait()
    tables(4, spots[4])
    stripes(0)
    stripes(1)
    for cross, passed in zip(x_cross, x_pass):
        cross.wait_recv()
        passed.start()
    project(3)
    hand_on_up(0)
    bring[2].wait()
    for copy in x_pass:
        copy.wait_recv()
    project(4)
    hand_on_up(1)
    lane = lanes((ROWS, 256))
    lane_pair = lane // 32 % 4
    lane_flat = lane // 64
    stat_lane = lanes((ROWS, 128))
    zero = jnp.zeros((), BF)

    def s_copy(g, slot, peer):
        return remote(stats.at[passing if slot == 4 else 0, g], stats.at[slot, g],
                      s_send.at[slot, g], s_recv.at[slot, g], peer)

    def d_copy(part, g):
        return remote(both.at[pl.ds(0, ROWS), cols(part, g)], both.at[pl.ds(ROWS, ROWS), cols(part, g)],
                      d_send.at[part, g], d_recv.at[part, g], partner)

    def send_first(s):
        px, lo = s // 6, lax.rem(s // 3, 2)

        @pl.when(px != x)
        def _():
            slot = lax.rem(px - x + 3, 4)
            remote(g_buf.at[s, pl.ds(0, 4)], in_x.at[slot, s - 6 * px], send_x.at[slot], recv_x.at[slot],
                   at(px, y, z, core)).start()

        for hi in range(2):
            py = hi * 2 + lo

            @pl.when(py != y)
            def _():
                slot = lax.rem(py - y + 3, 4)
                remote(g_buf.at[s, pl.ds(4, 4), hi], in_y.at[slot, px * 3 + lax.rem(s, 3)], send_y.at[slot],
                       recv_y.at[slot], at(x, py, z, core)).start()

    def weight_piece(part, g):
        d_copy(part, g).wait_recv()
        value = dot(xt[...], both[:, cols(part, g)]).astype(BF)
        first = part * 8 + g * 2
        g_buf[first] = value[:, :128].reshape(8, 2, 32, 128)
        g_buf[first + 1] = value[:, 128:].reshape(8, 2, 32, 128)
        send_first(first)
        send_first(first + 1)

    def pass_stats(g):
        s_copy(g, 2, pair).wait_recv()
        s_copy(g, 3, diagonal).wait_recv()
        s_copy(g, 4, partner).start()

    def out_copy(g):
        return pltpu.make_async_copy(out_ref.at[:, cols(0, g)], out_hbm.at[:, cols(0, g)], local.at[3 + g])

    @pl.loop(0, GROUPS)
    def _(g):
        mid = cols(0, g)
        query = qbuf[block(0), mid]
        up_g = upbuf[block(0), mid]
        out = jnp.zeros((ROWS, 256), F32)
        dquery = jnp.zeros((ROWS, 256), F32)
        ahead = dot_t(jnp.where(lane_pair == 0, query, zero), kbuf[:, mid])
        now = jnp.zeros((ROWS, 128), F32)
        for head in range(4):
            own_pair = lane_pair == head
            own_flat = lane_flat == head
            scores = ahead
            up_own = jnp.where(own_flat, up_g, zero)
            dprobs = dot_t(up_own, vbuf[:, mid])
            if head < 3:
                ahead = dot_t(jnp.where(lane_pair == head + 1, query, zero), kbuf[:, mid])
            row_max = None
            for slot in range(SLOTS):
                left = slot * ROWS
                one = jnp.maximum(scores[:, left:left + 128], scores[:, left + 128:left + 256]) - bias_to[slot]
                row_max = one if row_max is None else jnp.maximum(row_max, one)
            row_max = jnp.max(row_max, axis=1, keepdims=True)
            parts = []
            total = None
            for slot in range(SLOTS):
                one = jnp.exp2((scores[:, slot * ROWS:(slot + 1) * ROWS] - (row_max + bias_to[slot])) * LOG2E)
                part_sum = one[:, :128] + one[:, 128:]
                total = part_sum if total is None else total + part_sum
                parts.append(one)
            total = jnp.sum(total, axis=1, keepdims=True)
            weights = jnp.concatenate(parts, axis=1)
            inverse = 1.0 / total
            attended = dot(weights.astype(BF), vbuf[:, mid]) * inverse
            attended = attended.astype(BF).astype(F32)
            out = jnp.where(own_flat, attended, out)
            delta = jnp.sum(up_own.astype(F32) * attended, axis=1, keepdims=True)
            dscores = (weights * (dprobs - delta)).astype(BF)
            dquery = jnp.where(own_pair, dot(dscores, kbuf[:, mid]) * (inverse * 0.125), dquery)
            now = jnp.where(stat_lane == head, row_max * LOG2E + jnp.log2(total), now)
            now = jnp.where(stat_lane == head + 4, delta, now)
        stats[0, g] = now.T[:8]
        dquery = turn_back(dquery, cos5[0], sin5[0]).astype(BF)
        both[0:ROWS, mid] = dot_t(dquery, perm_ref[...]).astype(BF)
        out_ref[:, mid] = out.astype(BF)
        for slot, peer in routes:
            s_copy(g, slot, peer).start()
        d_copy(0, g).start()
        out_copy(g).start()

        @pl.when(g == 0)
        def _():
            hand_on_up(2)
            hand_on_up(3)

        @pl.when(g == 2)
        def _():
            for copy in u_cross:
                copy.wait_recv()
            u_pass.start()

        @pl.when(g > 0)
        def _():
            pass_stats(g - 1)
            weight_piece(0, g - 1)

    def gx_copy(j):
        return pltpu.make_async_copy(gx_ref.at[:, pl.ds(j * 256, 256)], gx_hbm.at[:, pl.ds(j * 256, 256)], local.at[7 + j])

    def grad_x(j):
        rows = slice(j * 256, (j + 1) * 256)
        gx_ref[:, rows] = dot_t(both[0:ROWS], wbuf[rows]).astype(BF)
        gx_copy(j).start()

    def nth(turn_no):
        return lax.rem(turn_no + lax.div(turn_no + 2, 3) + lax.div(turn_no, 3), GROUPS)

    @pl.loop(0, GROUPS)
    def _(turn_no):
        g = nth(turn_no)
        earlier = nth(lax.rem(turn_no + 3, GROUPS))
        mid = cols(0, g)
        s_copy(g, 1, partner).wait_recv()
        s_copy(g, 4, partner).wait_recv()

        @pl.when(turn_no == 0)
        def _():
            u_partner.wait_recv()
            u_pass.wait_recv()

        key, value = kbuf[block(0), mid], vbuf[block(0), mid]
        dkey = jnp.zeros((ROWS, 256), F32)
        dvalue = jnp.zeros((ROWS, 256), F32)
        for head in range(4):
            own_pair = lane_pair == head
            own_flat = lane_flat == head
            lse = jnp.concatenate([stats[slot, g, head:head + 1] + bias_from[slot] for slot in range(SLOTS)], axis=1)
            delta = jnp.concatenate([stats[slot, g, head + 4:head + 5] for slot in range(SLOTS)], axis=1)
            scores = dot_t(jnp.where(own_pair, key, zero), qbuf[:, mid]) * LOG2E
            probs = jnp.exp2(scores - lse)
            dprobs = dot_t(jnp.where(own_flat, value, zero), upbuf[:, mid])
            dscores = (probs * (dprobs - delta)).astype(BF)
            dvalue = jnp.where(own_flat, dot(probs.astype(BF), upbuf[:, mid]), dvalue)
            dkey = jnp.where(own_pair, dot(dscores, qbuf[:, mid]), dkey)
            if head == 2:
                @pl.when(turn_no == 0)
                def _():
                    pass_stats(GROUPS - 1)
                    weight_piece(0, GROUPS - 1)

                @pl.when(turn_no > 0)
                def _():
                    weight_piece(2, earlier)
                    weight_piece(1, earlier)
        dkey = turn_back(dkey, cos5[0], sin5[0]).astype(BF)
        both[0:ROWS, cols(2, g)] = dvalue.astype(BF)
        both[0:ROWS, cols(1, g)] = dot_t(dkey, perm_ref[...]).astype(BF)
        d_copy(2, g).start()
        d_copy(1, g).start()

    grad_x(0)
    weight_piece(2, 1)
    weight_piece(1, 1)

    grad_x(1)
    first_a = [remote(in_x.at[i], in_x.at[i], send_x.at[i], recv_x.at[i], at(p, y, z, core)) for i, p in enumerate(x_peers)]
    first_b = [remote(in_y.at[i], in_y.at[i], send_y.at[i], recv_y.at[i], at(x, p, z, core)) for i, p in enumerate(y_peers)]
    for copy in first_a:
        copy.wait_recv()
    for j in range(6):
        total = g_buf[6 * x + j, 0:4].astype(F32)
        for i in range(3):
            total += in_x[i, j].astype(F32)
        sum_a[j] = total.astype(BF)
    second_a = [remote(sum_a.at[pl.ds(lax.rem(p, 2) * 3, 3), :, p // 2], in_a.at[i], send_a.at[i], recv_a.at[i],
                       at(x, p, z, core)) for i, p in enumerate(y_peers)]
    for copy in second_a:
        copy.start()
    for copy in first_b:
        copy.wait_recv()
    for px in range(4):
        for j in range(3):
            total = g_buf[px * 6 + y_lo * 3 + j, 4:8, y_hi].astype(F32)
            for i in range(3):
                total += in_y[i, px * 3 + j].astype(F32)
            sum_b[px * 3 + j] = total.astype(BF)
    second_b = [remote(sum_b.at[pl.ds(p * 3, 3)], in_b.at[i], send_b.at[i], recv_b.at[i], at(p, y, z, core))
                for i, p in enumerate(x_peers)]
    for copy in second_b:
        copy.start()
    grad_x(2)
    for copy in second_a:
        copy.wait_recv()
    def halves(rows, blocks):
        middle = blocks[1].astype(BF).astype(F32)
        for c in range(2):
            part = middle[:, :, c * 64:(c + 1) * 64]
            sum_p[rows, c, 0:32] = blocks[2 * c].astype(BF)
            sum_p[rows, c, 32:48] = jnp.concatenate([part[:, :16], part[:, 16:]], axis=2).astype(BF)

    third = [(z, remote(sum_p.at[z, 1 - core], in_z.at[0, core], send_z.at[0, 1 - core], recv_z.at[0, core], partner))]
    for i, p in enumerate(z_peers):
        for c in range(2):
            third.append((p, remote(sum_p.at[p, c], in_z.at[i + 1, core], send_z.at[i + 1, c], recv_z.at[i + 1, core],
                                    at(x, y, p, c))))

    def send_third(upper):
        for p, copy in third:
            @pl.when(p // 4 == upper)
            def _():
                copy.start()

    blocks = []
    for j in range(3):
        total = sum_a[y_lo * 3 + j, :, y_hi].astype(F32)
        for i in range(3):
            total += in_a[i, j].astype(F32)
        blocks.append(total)
    halves(slice(0, 4), blocks)
    send_third(0)
    for copy in second_b:
        copy.wait_recv()
    blocks = []
    for j in range(3):
        total = sum_b[x * 3 + j].astype(F32)
        for i in range(3):
            total += in_b[i, j].astype(F32)
        blocks.append(total)
    halves(slice(4, 8), blocks)
    send_third(1)
    grad_x(3)
    for copy in first_a + first_b + second_a + second_b + x_pair + x_cross + x_pass + u_pair + u_cross + [u_partner, u_pass]:
        copy.wait_send()

    @pl.loop(0, GROUPS)
    def _(g):
        for part in range(3):
            d_copy(part, g).wait_send()
        s_copy(g, 1, partner).wait_send()
        s_copy(g, 2, pair).wait_send()
        s_copy(g, 3, diagonal).wait_send()
        s_copy(g, 4, partner).wait_send()
        out_copy(g).wait()

    for j in range(4):
        gx_copy(j).wait()
    for _, copy in third:
        copy.wait_send()

    def arrived(i, c):
        remote(in_z.at[i, c], in_z.at[i, c], send_z.at[i, c], recv_z.at[i, c], partner).wait_recv()

    give = []
    for own in (False, True):
        c = core if own else 1 - core
        total = None
        for i in range(8):
            if own and i == 0:
                one = sum_p[z, core]
            else:
                arrived(i, c)
                one = in_z[i, c]
            total = one.astype(F32) if total is None else total + one.astype(F32)
        total = total * (65536.0 ** -0.5)
        whole = total[:32]
        middle = jnp.concatenate([total[32:, :64], total[32:, 64:]], axis=0)
        gw_ref[pl.ds(pl.multiple_of(c * 32, 32), 32), :] = jnp.where(
            core == 0, jnp.concatenate([whole, middle], axis=1), jnp.concatenate([middle, whole], axis=1))
        done = pl.ds(pl.multiple_of(c * 32, 32), 32)
        give.append(pltpu.make_async_copy(gw_ref.at[done], gw_hbm.at[done], local.at[13 + own]))
        give[-1].start()
    for copy in give:
        copy.wait()


def run_step(listed, x, w, up, spots):
    hbm = pl.BlockSpec(memory_space=pl.ANY)
    dma = pltpu.SemaphoreType.DMA
    block = jax.ShapeDtypeStruct((ROWS, 1024), BF)
    buffers = [
        ((ROWS, 1024), BF), ((ROWS, 1024), BF), ((64, 192), F32),
        ((256, 256), BF), ((SLOTS, ROWS, 1024), BF), ((SLOTS, 1, ROWS), jnp.int32), ((1024, 3072), BF), ((1024, 2048), BF),
        ((SLOTS * ROWS, 1024), BF), ((SLOTS * ROWS, 1024), BF), ((SLOTS * ROWS, 1024), BF), ((SLOTS * ROWS, 1024), BF),
        ((SLOTS, ROWS, 128), F32), ((SLOTS, ROWS, 128), F32), ((SLOTS, GROUPS, 8, ROWS), F32),
        ((2 * ROWS, 3072), BF), ((512, 512), BF),
        ((24, 8, 2, 32, 128), BF), ((3, 6, 4, 2, 32, 128), BF), ((3, 12, 4, 32, 128), BF), ((6, 4, 2, 32, 128), BF),
        ((12, 4, 32, 128), BF), ((3, 3, 4, 32, 128), BF), ((3, 3, 4, 32, 128), BF), ((8, 2, 48, 128), BF),
        ((8, 2, 48, 128), BF),
    ]
    x_moves, u_moves = (2 + 3 * PIECES,), (2 + 2 * PIECES,)
    semaphores = [dma((15,)), dma(x_moves), dma(x_moves), dma((5,)), dma((5,)), dma(u_moves), dma(u_moves)]
    semaphores += [dma((5, GROUPS))] * 2 + [dma((3, GROUPS))] * 2 + [dma((3,))] * 8 + [dma((8, 2))] * 2
    return pl.pallas_call(
        step_kernel,
        in_specs=[hbm] * 5,
        out_specs=[hbm] * 3,
        out_shape=[block, block, jax.ShapeDtypeStruct((64, 192), F32)],
        scratch_shapes=[pltpu.SMEM((1, 5), jnp.int32)] + [pltpu.VMEM(shape, kind) for shape, kind in buffers] + semaphores,
        compiler_params=pltpu.CompilerParams(collective_id=0, has_side_effects=True, vmem_limit_bytes=63 * 2**20),
        name="whole_step",
    )(listed, x, w, up, spots)


def hand_out_kernel(a_hbm, b_hbm, c_hbm, a_out, b_out, c_out, a_buf, b_buf, c_buf, sems):
    moves = []
    for source, buffer, target, parts in ((a_hbm, a_buf, a_out, 4), (b_hbm, b_buf, b_out, 4), (c_hbm, c_buf, c_out, 1)):
        rows = buffer.shape[0] // parts
        for i in range(parts):
            part = pl.ds(i * rows, rows)
            sem = sems.at[len(moves)]
            moves.append((pltpu.make_async_copy(source.at[part], buffer.at[part], sem),
                          pltpu.make_async_copy(buffer.at[part], target.at[part], sem)))
    for bring, _ in moves:
        bring.start()
    for bring, give in moves:
        bring.wait()
        give.start()
    for _, give in moves:
        give.wait()


def hand_out(a, b, c):
    hbm = pl.BlockSpec(memory_space=pl.ANY)
    arrays = (a, b, c)
    return pl.pallas_call(
        hand_out_kernel,
        in_specs=[hbm] * 3,
        out_specs=[hbm] * 3,
        out_shape=[jax.ShapeDtypeStruct(one.shape, one.dtype) for one in arrays],
        scratch_shapes=[pltpu.VMEM(one.shape, one.dtype) for one in arrays] + [pltpu.SemaphoreType.DMA((9,))],
        name="hand_out",
    )(*arrays)


def per_device(features, w_qkv, grad_out, positions, block_list):
    out, grad_x, grad_w = hand_out(*run_step(block_list, features[0], w_qkv, grad_out[0], positions))
    return (out[None], grad_x[None], grad_w)


def solution(mesh):
    return jax.shard_map(
        per_device,
        mesh=mesh,
        in_specs=(
            P("dates", "lon", None),
            P(),
            P("dates", "lon", None),
            P("dates", "lon"),
            P("dates", None),
        ),
        out_specs=(P("dates", "lon", None), P("dates", "lon", None), P("dates", "lon")),
        check_vma=False,
    )
```
